32 devices in a mesh: groups: 2 (over y), seq: 16 (over z, x, core).
Axes of the slice: x: 2, y: 2, z: 4, core: 2. Of those that a mesh axis runs over, the one named last changes fastest.
Arguments:
- queries: bfloat16 [8192, 2048], P(('groups', 'seq')), parts along dimension 0, may hold values from -6 to 6
- keys: bfloat16 [8192, 2048], P(('groups', 'seq')), parts along dimension 0, may hold values from -0.5390625 to 0.5390625
- values: bfloat16 [8192, 2048], P(('groups', 'seq')), parts along dimension 0, may hold values from -6 to 6
- prompt_state: bfloat16 [16, 2048, 128], P('groups', 'seq'), parts along dimension 0, may hold values from -12 to 12
- lengths: int32 [16], P('groups'), parts along dimension 0, may hold values from 1 to 16, 32 in all
- prompt_of: int32 [16, 1], P('groups'), parts along dimension 0, may hold values from 0 to 7
Outputs:
- mixed: bfloat16 [8192, 2048], P(('groups', 'seq')), parts along dimension 0
The draws below stay inside these ranges and needn't reach their ends.
There are 2 independent parts, one for each index of `groups`. The reference program is written for one: setup_inputs(seed, part) draws one part's arguments, and reference() takes and returns one part's arrays. A program takes and returns all parts, laid end to end along the dimension named above; each array names one. Nothing has to cross between parts.
Inputs may be any that keep to these rules, and one draw needn't show every extreme that they name: `lengths`: responses fill the group's blocks exactly in order; the longest has exactly 16 blocks. `prompt_of`: every prompt has exactly one response.
All inputs are finite; a program needn't handle non-finite values.
Results may differ from the reference program's by a relative error of at most 0.0046.
Values may be sent and summed in bfloat16 or wider, within the bound.
A program may use at most 64 MiB of HBM per device.

```python
import math
import jax
import jax.numpy as jnp
import numpy as np
from jax import lax

H = 16
DK = 128
DV = 128
SPAN = 128
PROMPTS = 8
TOKENS = 4096
RESP = 8
MOST = 16


def block_scale(rng, shape, shards, smallest, top_value):
    level, own = 1.0, jax.random.fold_in(rng, 6)
    for axis_at, parts in shards:
        draws = jnp.exp(jax.random.uniform(jax.random.fold_in(own, axis_at), (parts,), jnp.float32, smallest / len(shards), top_value / len(shards)))
        level = level * jnp.repeat(draws, shape[axis_at] // parts).reshape([-1 if axis == axis_at else 1 for axis in range(len(shape))])
    return level


def different_ones(stream_key, rows, number_of, top, lift):
    sequence = jax.random.permutation(jax.random.fold_in(stream_key, 1), number_of)
    boost = sequence
    for power in range(3):
        boost = boost * boost // number_of
    boost = boost * lift // number_of
    lots = jax.random.randint(jax.random.fold_in(stream_key, 2), (rows, number_of), 0, 4096) + boost
    sure = jax.random.permutation(jax.random.fold_in(stream_key, 3), rows)[jnp.arange(number_of) % rows]
    lots = jnp.where(jnp.arange(rows)[:, None] == sure[None, :], 1 << 14, lots)
    priority = lots * number_of + jnp.arange(number_of)
    return lax.top_k(priority.astype(jnp.int32), top)[1].astype(jnp.int32)


def profile(number_of, total, limit, skew):
    portions = [(1 << 20) // math.isqrt(rank ** skew) + 1 for rank in range(2, number_of + 1)]
    surplus, holding = total - limit - (number_of - 1), [1] * (number_of - 1)
    while surplus > 0:
        movable = [i for i in range(number_of - 1) if holding[i] < limit]
        whole, remaining = sum([portions[i] for i in movable]), surplus
        for i in movable:
            extra = min(limit - holding[i], max(1, remaining * portions[i] // whole), surplus)
            holding[i] = holding[i] + extra
            surplus = surplus - extra
    return np.array([limit] + holding)


def uneven_parts(rng, amount, total, limit, lean):
    if amount == 2:
        one = jax.random.randint(rng, (), max(1, total - limit), min(limit, total - 1) + 1)
        return jnp.stack([one, total - one])
    tallies = jnp.asarray(profile(amount, total, limit, lean), jnp.int32)
    pairs = (amount - 1) // 2
    giver, taker = tallies[1:1 + 2 * pairs:2], tallies[2:2 + 2 * pairs:2]
    margin = jnp.minimum(giver - 1, limit - taker)
    moved = jax.random.randint(jax.random.fold_in(rng, 1), (pairs,), 0, 1 << 20) % (margin + 1)
    tallies = tallies.at[1:1 + 2 * pairs:2].set(giver - moved).at[2:2 + 2 * pairs:2].set(taker + moved)
    return tallies[jax.random.permutation(jax.random.fold_in(rng, 2), amount)]


def scatter_about(own_key, extent, scale, most, shards=(), kind=jnp.bfloat16):
    factor_of = block_scale(own_key, extent, shards, -0.22, 0.18) if shards else 1.0
    array = jax.random.normal(own_key, extent, jnp.float32) * scale * factor_of
    return jnp.minimum(jnp.maximum(array, -most), most).astype(kind)


def setup_inputs(seed: int = 0, part: int = 0) -> dict:
    key_of = jax.random.split(jax.random.key(seed), 7)
    own_keys = jax.random.split(jax.random.fold_in(key_of[6], part), 7)
    return {
        "queries": scatter_about(own_keys[0], (TOKENS, H * DK), 1.0, 6.0, ((0, 16),)),
        "keys": scatter_about(own_keys[1], (TOKENS, H * DK), 0.09, 0.5390625, ((0, 16),)),
        "values": scatter_about(own_keys[2], (TOKENS, H * DV), 1.0, 6.0, ((0, 16),)),
        "prompt_state": scatter_about(own_keys[3], (PROMPTS, H * DK, DV), 2.0, 12.0, ((1, 16),)),
        "lengths": uneven_parts(own_keys[4], RESP, TOKENS // SPAN, MOST, 2).astype(jnp.int32),
        "prompt_of": different_ones(own_keys[5], RESP, PROMPTS, 1, 0),
    }


epsilon = 1e-06

def normalize(mixed):
    scale = lax.rsqrt(lax.optimization_barrier(jnp.mean(mixed * mixed, axis=-1, keepdims=True)) + epsilon)
    return mixed * scale

def reference(queries, keys, values, prompt_state, lengths, prompt_of):
    blocks = TOKENS // SPAN
    starts = (jnp.cumsum(lengths) - lengths).astype(jnp.int32)
    block_ids = jnp.arange(blocks, dtype=jnp.int32)
    hits = (starts[None, :] == block_ids[:, None]).astype(jnp.int32)
    is_start = lax.optimization_barrier(jnp.sum(hits, axis=1)) > 0
    block_prompt = lax.optimization_barrier(jnp.sum(hits * prompt_of[:, 0][None, :], axis=1)).astype(jnp.int32)
    query_blocks = queries.reshape(blocks, SPAN, H, DK)
    key_blocks = keys.reshape(blocks, SPAN, H, DK)
    value_blocks = values.reshape(blocks, SPAN, H, DV)
    causal = jnp.tril(jnp.ones((SPAN, SPAN), dtype=bool))
    highest = lax.Precision.HIGHEST

    def advance(carried, inputs):
        query_part, key_part, value_part, starting, which = inputs
        cached = lax.dynamic_index_in_dim(prompt_state, which, 0, keepdims=False)
        cached = cached.astype(jnp.float32).reshape(H, DK, DV)
        state = jnp.where(starting, cached, carried)
        query_wide = query_part.astype(jnp.float32)
        key_wide = key_part.astype(jnp.float32)
        value_wide = value_part.astype(jnp.float32)
        rounded = lax.optimization_barrier(state.astype(jnp.bfloat16)).astype(jnp.float32)
        inter = jnp.einsum('thd,hde->the', query_wide, rounded, precision=highest)
        scores = jnp.einsum('thd,shd->hts', query_wide, key_wide, precision=highest)
        masked = jnp.where(causal[None], scores, jnp.float32(0.0))
        weights = lax.optimization_barrier(masked.astype(jnp.bfloat16)).astype(jnp.float32)
        intra = jnp.einsum('hts,she->the', weights, value_wide, precision=highest)
        mixed = normalize(inter + intra).astype(jnp.bfloat16).reshape(SPAN, H * DV)
        updated = state + jnp.einsum('thd,the->hde', key_wide, value_wide, precision=highest)
        return (updated, mixed)
    initial = jnp.zeros((H, DK, DV), dtype=jnp.float32)
    _, outputs = lax.scan(advance, initial, (query_blocks, key_blocks, value_blocks, is_start, block_prompt))
    return outputs.reshape(TOKENS, H * DV)
```

```python
import functools
import jax
import jax.numpy as jnp
from jax import lax
from jax.experimental import pallas as pl
from jax.experimental.pallas import tpu as pltpu
from jax.sharding import PartitionSpec as P

DK = 128
DV = 128
SPAN = 128
epsilon = 1e-06


def matmul(a, b, ca, cb):
    return lax.dot_general(a, b, (((ca,), (cb,)), ((), ())), preferred_element_type=jnp.float32)


def kernel(n, q_hbm, k_hbm, v_hbm, p_hbm, len_ref, of_ref, out_hbm,
           q_ref, k_ref, v_ref, own_prompts, far_prompts, out_ref, intra, first, sum_out, sum_in, st_out, st_in, pr_out, pr_in,
           over_out, over_in, index, flag, load_sem, out_sem, swap_sem, over_send, over_recv, sum_send, sum_recv, st_send, st_recv,
           pr_send, pr_recv):
    me = lax.axis_index("seq")
    half = n // 2
    side = me // half
    own = lax.rem(me, half)
    base = side * half
    partner = lax.rem(me + half, n)
    width = k_ref.shape[1]
    heads = width // DK
    rows = width // n
    pieces = DK // rows
    responses = len_ref.shape[0]

    def load(i, src, dst):
        return pltpu.make_async_copy(src, dst, load_sem.at[i])

    loads = [load(0, p_hbm, own_prompts), load(1, k_hbm, k_ref), load(2, v_hbm, v_ref), load(3, q_hbm, q_ref)]
    for copy in loads:
        copy.start()

    barrier = pltpu.get_barrier_semaphore()

    def greet(device):
        pl.semaphore_signal(barrier, inc=1, device_id={"seq": device}, device_id_type=pl.DeviceIdType.MESH)

    greet(partner)

    @pl.loop(1, half)
    def _(j):
        greet(base + lax.rem(own + j, half))

    @pl.loop(0, n)
    def _(i):
        c = 2 * base + i
        start = jnp.int32(0)
        begins = jnp.int32(0)
        which = jnp.int32(0)
        for r in range(responses):
            hit = jnp.where(start == c, 1, 0)
            begins = begins + hit
            which = which + hit * of_ref[r]
            start = start + len_ref[r]
        flag[i] = begins
        index[i] = which

    pl.semaphore_wait(barrier, half)

    def send(src, dst, send_sem, recv_sem, target):
        return pltpu.make_async_remote_copy(
            src_ref=src, dst_ref=dst, send_sem=send_sem, recv_sem=recv_sem,
            device_id={"seq": target}, device_id_type=pl.DeviceIdType.MESH)

    loads[0].wait()
    swap = send(own_prompts, far_prompts, swap_sem.at[0], swap_sem.at[1], partner)
    swap.start()

    def give_prompts(slot, prompts):
        @pl.loop(1, half + 1)
        def _(j):
            target = lax.rem(own + j, half)
            pr_out[target, slot] = prompts[index[2 * target + 1]]

            @pl.when(target != own)
            def _():
                send(pr_out.at[target, slot], pr_in.at[own, slot], pr_send, pr_recv.at[slot], base + target).start()

        pr_in[own, slot] = pr_out[own, slot]

    loads[1].wait()
    loads[2].wait()
    second_starts = flag[2 * own + 1] > 0

    @pl.loop(0, heads // 2)
    def _(i):
        pair = lax.rem(own // pieces + 1 + i, heads // 2)
        for slot in range(2):
            h = pair + lax.rem(side + slot, 2) * (heads // 2)
            cols = pl.ds(pl.multiple_of(h * DK, DK), DK)
            a = matmul(k_ref[0:SPAN, cols], v_ref[0:SPAN, cols], 0, 0)
            b = matmul(k_ref[SPAN:2 * SPAN, cols], v_ref[SPAN:2 * SPAN, cols], 0, 0)
            first[h] = a
            total = jnp.where(second_starts, b, a + b).astype(jnp.bfloat16)
            for j in range(pieces):
                sum_out[pair * pieces + j, slot] = total[j * rows:(j + 1) * rows]
        for j in range(pieces):
            owner = pair * pieces + j

            @pl.when(owner != own)
            def _():
                send(sum_out.at[owner], sum_in.at[own], sum_send, sum_recv.at[own], base + owner).start()

    sum_in[own] = sum_out[own]

    loads[3].wait()
    causal = lax.broadcasted_iota(jnp.int32, (SPAN, SPAN), 0) >= lax.broadcasted_iota(jnp.int32, (SPAN, SPAN), 1)

    def within(low, high):
        @pl.loop(low, high, step=4)
        def _(group):
            parts = []
            for u in range(4):
                cols = pl.ds(pl.multiple_of((group + u) * DK, DK), DK)
                for block in range(2):
                    parts.append((slice(block * SPAN, (block + 1) * SPAN), cols))
            weights = [jnp.where(causal, matmul(q_ref[rng, cols], k_ref[rng, cols], 1, 1), 0.0).astype(jnp.bfloat16) for rng, cols in parts]
            for (rng, cols), weight in zip(parts, weights):
                intra[rng, cols] = matmul(weight, v_ref[rng, cols], 1, 0)

    def sums_arrived():
        @pl.loop(1, half)
        def _(j):
            d = lax.rem(own + half - j, half)
            send(sum_out.at[d], sum_in.at[d], sum_send, sum_recv.at[d], base + d).wait_recv()

    def scan(slot, prompts, state):
        def step(d, state):
            state = jnp.where(flag[2 * d] > 0, prompts[index[2 * d]].astype(jnp.float32), state)
            st_out[d, slot] = state.astype(jnp.bfloat16)
            state = jnp.where(flag[2 * d + 1] > 0, prompts[index[2 * d + 1]].astype(jnp.float32), state)
            return state + sum_in[d, slot].astype(jnp.float32)

        return lax.fori_loop(0, half, step, state)

    def give_states(slot):
        @pl.loop(1, half)
        def _(j):
            d = lax.rem(own + j, half)
            send(st_out.at[d, slot], st_in.at[own, slot], st_send, st_recv.at[slot, own], base + d).start()

        st_in[own, slot] = st_out[own, slot]

    def over(slot):
        return send(over_out.at[slot], over_in.at[1 - slot], over_send.at[slot], over_recv.at[1 - slot], partner)

    def arrived(slot):
        over(1 - slot).wait_recv()
        return over_in[slot].astype(jnp.float32)

    def hand_over(slot, state):
        over_out[slot] = state.astype(jnp.bfloat16)
        over(slot).start()

    nothing = jnp.zeros((rows, DV), jnp.float32)

    give_prompts(0, own_prompts)
    within(0, heads)
    sums_arrived()

    @pl.when(side == 0)
    def _():
        hand_over(0, scan(0, own_prompts, nothing))
        give_states(0)
        swap.wait_recv()
        hand_over(1, scan(1, far_prompts, nothing))
        give_prompts(1, far_prompts)
        give_states(1)

    @pl.when(side == 1)
    def _():
        swap.wait_recv()
        give_prompts(1, far_prompts)
        scan(1, far_prompts, arrived(1))
        give_states(1)
        scan(0, own_prompts, arrived(0))
        give_states(0)

    def others(ref):
        return ref.at[0:half - 1]

    @pl.loop(0, 2)
    def _(turn):
        slot = lax.rem(side + turn, 2)
        pltpu.make_async_copy(pr_in.at[0:half - 1, 0], pr_in.at[0:half - 1, 0], pr_recv.at[slot]).wait()

        @pl.loop(0, heads // 2)
        def _(i):
            pair = lax.rem(own // pieces + heads // 2 - i, heads // 2)
            for j in range(pieces):
                owner = pair * pieces + j

                @pl.when(owner != own)
                def _():
                    send(st_out.at[owner, slot], st_in.at[owner, slot], st_send, st_recv.at[slot, owner], base + owner).wait_recv()

            h = pair + lax.rem(side + slot, 2) * (heads // 2)
            cols = pl.ds(pl.multiple_of(h * DK, DK), DK)
            entering = st_in[pl.ds(pair * pieces, pieces), slot].reshape(DK, DV)
            prompt = pr_in[pl.ds(pair * pieces, pieces), slot].reshape(DK, DV)
            later = (entering.astype(jnp.float32) + first[h]).astype(jnp.bfloat16)
            states = (entering, jnp.where(second_starts, prompt, later))
            for block in range(2):
                rng = slice(block * SPAN, (block + 1) * SPAN)
                o = matmul(q_ref[rng, cols], states[block], 1, 0) + intra[rng, cols]
                scale = lax.rsqrt(jnp.mean(o * o, axis=-1, keepdims=True) + epsilon)
                out_ref[rng, cols] = (o * scale).astype(jnp.bfloat16)
            pltpu.make_async_copy(out_ref.at[:, cols], out_hbm.at[:, cols], out_sem).start()

    pltpu.make_async_copy(out_ref, out_hbm, out_sem).wait()
    swap.wait_send()
    pltpu.make_async_copy(others(pr_out), others(pr_out), pr_send).wait()
    pltpu.make_async_copy(others(sum_out), others(sum_out), sum_send).wait()
    pltpu.make_async_copy(others(st_out), others(st_out), st_send).wait()

    @pl.when(side == 0)
    def _():
        over(0).wait_send()
        over(1).wait_send()


def solution(mesh):
    n = mesh.shape["seq"]

    def shards(queries, keys, values, prompt_state, lengths, prompt_of):
        tokens, width = queries.shape
        prompts, rows, _ = prompt_state.shape
        half = jnp.bfloat16
        anywhere = pl.BlockSpec(memory_space=pl.ANY)
        scalar = pl.BlockSpec(memory_space=pltpu.SMEM)
        piece = pltpu.VMEM((n // 2, 2, rows, DV), half)
        dma = pltpu.SemaphoreType.DMA
        return pl.pallas_call(
            functools.partial(kernel, n),
            out_shape=jax.ShapeDtypeStruct((tokens, width), half),
            in_specs=[anywhere] * 4 + [scalar] * 2,
            out_specs=anywhere,
            scratch_shapes=[
                pltpu.VMEM((tokens, width), half),
                pltpu.VMEM((tokens, width), half),
                pltpu.VMEM((tokens, width), half),
                pltpu.VMEM((prompts, rows, DV), half),
                pltpu.VMEM((prompts, rows, DV), half),
                pltpu.VMEM((tokens, width), half),
                pltpu.VMEM((tokens, width), jnp.float32),
                pltpu.VMEM((width // DK, DK, DV), jnp.float32),
                piece, piece, piece, piece, piece, piece,
                pltpu.VMEM((2, rows, DV), half),
                pltpu.VMEM((2, rows, DV), half),
                pltpu.SMEM((n,), jnp.int32),
                pltpu.SMEM((n,), jnp.int32),
                dma((4,)), dma(()), dma((2,)), dma((2,)), dma((2,)),
                dma(()), dma((n // 2,)), dma(()), dma((2, n // 2)), dma(()), dma((2,)),
            ],
            compiler_params=pltpu.CompilerParams(
                collective_id=0, has_side_effects=True, vmem_limit_bytes=62 << 20),
        )(queries, keys, values, prompt_state, lengths, prompt_of.reshape(-1))

    placed = (
        P(("groups", "seq"), None),
        P(("groups", "seq"), None),
        P(("groups", "seq"), None),
        P("groups", "seq", None),
        P("groups"),
        P("groups", None),
    )
    return jax.shard_map(
        shards, mesh=mesh, in_specs=placed, out_specs=P(("groups", "seq"), None), check_vma=False
    )
```

```python
import functools
import jax
import jax.numpy as jnp
from jax import lax
from jax.experimental import pallas as pl
from jax.experimental.pallas import tpu as pltpu
from jax.sharding import PartitionSpec as P

DK = 128
DV = 128
SPAN = 128
epsilon = 1e-06


def matmul(a, b, ca, cb):
    return lax.dot_general(a, b, (((ca,), (cb,)), ((), ())), preferred_element_type=jnp.float32)


def plane_width(n):
    x = 1
    while (2 * x) ** 3 <= n // 2:
        x *= 2
    return 2 * x


def kernel(n, q_hbm, k_hbm, v_hbm, p_hbm, len_ref, of_ref, out_hbm,
           q_ref, k_ref, v_ref, prompts, out_ref, intra, first, gathered, t_out, t_in, s_out, s_in, enter, d_out, d_in, flag, index,
           ready_up, ready_mate, load_sem, out_sem, g_send, g_recv, t_send, t_recv, s_send, s_recv, d_send, d_recv):
    me = lax.axis_index("seq")
    w = plane_width(n)
    planes = n // w
    z = me // w
    j = lax.rem(me, w)
    upper = 2 * z >= planes
    heads = k_ref.shape[1] // DK
    rows = prompts.shape[1]
    pieces = DK // rows
    per_level = w // pieces
    _, chunks, responses, part, _ = gathered.shape
    some = responses - 1

    def load(i, src, dst):
        return pltpu.make_async_copy(src, dst, load_sem.at[i])

    loads = [load(0, p_hbm, prompts), load(1, k_hbm, k_ref), load(2, v_hbm, v_ref), load(3, q_hbm, q_ref)]
    for copy in loads:
        copy.start()

    def signal(sem, device):
        pl.semaphore_signal(sem, inc=1, device_id={"seq": device}, device_id_type=pl.DeviceIdType.MESH)

    def send(src, dst, send_sem, recv_sem, target):
        return pltpu.make_async_remote_copy(
            src_ref=src, dst_ref=dst, send_sem=send_sem, recv_sem=recv_sem,
            device_id={"seq": target}, device_id_type=pl.DeviceIdType.MESH)

    def pass_by(sem, ref):
        return pltpu.make_async_copy(ref, ref, sem)

    barrier = pltpu.get_barrier_semaphore()
    has_up = z < planes - 1
    has_down = z > 0

    @pl.when(has_up)
    def _():
        signal(barrier, me + w)

    @pl.loop(j + 1, w)
    def _(m):
        signal(barrier, z * w + m)

    @pl.when(me > 0)
    def _():
        pl.semaphore_wait(barrier, j + jnp.where(has_down, 1, 0))

    @pl.when(has_down)
    def _():
        signal(ready_up, me - w)

    @pl.loop(0, j)
    def _(m):
        signal(ready_mate, z * w + m)

    def hop(level, c, up):
        target = jnp.where(up, me + w, me - w)
        target_upper = 2 * jnp.where(up, z + 1, z - 1) >= planes

        def go(low, count):
            ref = gathered.at[level, c, pl.ds(low, count)]
            send(ref, ref, g_send.at[level, int(up)], g_recv.at[level, c], target).start()

        @pl.when(target_upper != up)
        def _():
            go(0, responses)

        @pl.when(target_upper == up)
        def _():
            go(int(up), some)

    def hop_sent(level, up):
        target_upper = 2 * jnp.where(up, z + 1, z - 1) >= planes

        @pl.when(target_upper != up)
        def _():
            pass_by(g_send.at[level, int(up)], gathered.at[level]).wait()

        @pl.when(target_upper == up)
        def _():
            pass_by(g_send.at[level, int(up)], gathered.at[level, :, pl.ds(int(up), some)]).wait()

    def hop_arrived(level, c, up):
        @pl.when(upper != up)
        def _():
            pass_by(g_recv.at[level, c], gathered.at[level, c]).wait()

        @pl.when(upper == up)
        def _():
            pass_by(g_recv.at[level, c], gathered.at[level, c, pl.ds(int(up), some)]).wait()

    loads[0].wait()
    for r in range(responses):
        gathered[z, :, r] = prompts[of_ref[r]].reshape(chunks, part, DV)

    @pl.when(has_down)
    def _():
        for c in range(chunks):
            hop(z, c, False)

    @pl.loop(0, 2 * w)
    def _(i):
        c = 2 * z * w + i
        start = jnp.int32(0)
        begins = jnp.int32(0)
        which = jnp.int32(-1)
        for r in range(responses):
            begins = begins + jnp.where(start == c, 1, 0)
            which = which + jnp.where(start <= c, 1, 0)
            start = start + len_ref[r]
        flag[i] = begins
        index[i] = which

    @pl.when(z == 0)
    def _():
        s_in[...] = jnp.zeros_like(s_in)

    second_starts = flag[2 * j + 1] > 0
    group = 4

    def columns(h):
        return pl.ds(pl.multiple_of(h * DK, DK), DK)

    loads[1].wait()
    loads[2].wait()

    @pl.loop(0, heads, step=group)
    def _(base):
        for u in range(group):
            h = base + u
            cols = columns(h)
            a = matmul(k_ref[0:SPAN, cols], v_ref[0:SPAN, cols], 0, 0)
            b = matmul(k_ref[SPAN:2 * SPAN, cols], v_ref[SPAN:2 * SPAN, cols], 0, 0)
            first[h] = a
            total = jnp.where(second_starts, b, a + b).astype(jnp.bfloat16)
            for p in range(pieces):
                g = h * pieces + p
                t_out[lax.rem(g, w), g // w] = total[p * rows:(p + 1) * rows]

    t_in[j] = t_out[j]

    @pl.when(j < w - 1)
    def _():
        pl.semaphore_wait(ready_mate, w - 1 - j)

    @pl.loop(0, planes)
    def _(level):
        for k in range(1, w):
            m = lax.rem(j + k, w)
            send(t_out.at[m, level], t_in.at[j, level], t_send, t_recv.at[j, level], z * w + m).start()

    @pl.when(has_up)
    def _():
        pl.semaphore_wait(ready_up, 1)
        for c in range(chunks):
            hop(z, c, True)

    low = jnp.where(upper, 1, 0)

    def prompt(level, c, block):
        which = index[block]
        chosen = gathered[level, c, low]
        for r in range(1, some):
            chosen = jnp.where(which == low + r, gathered[level, c, low + r], chosen)
        return chosen

    def make(level, c, second):
        for k in range(w):
            m = lax.rem(j + k, w)
            ref = d_in.at[level, j] if k == 0 else d_out.at[level, m]
            if second:
                ref[c, 1] = prompt(level, c, 2 * m + 1)
            else:
                entering = enter[level, m, c * part:(c + 1) * part] if isinstance(c, int) else enter[level, m, pl.ds(pl.multiple_of(c * part, part), part)]
                ref[c, 0] = (prompt(level, c, 2 * m).astype(jnp.float32) + entering).astype(jnp.bfloat16)

    def give(level, where):
        for k in range(1, w):
            m = lax.rem(j + k, w)
            send(d_out.at[level, m].at[where], d_in.at[level, j].at[where], d_send, d_recv.at[level, j], z * w + m).start()

    def seconds(level):
        for c in range(chunks):
            make(level, c, True)
        give(level, (slice(None), 1))

    def states(level):
        for c in range(chunks):
            make(level, c, False)
        give(level, (slice(None), 0))

    seconds(z)

    loads[3].wait()
    causal = lax.broadcasted_iota(jnp.int32, (SPAN, SPAN), 0) >= lax.broadcasted_iota(jnp.int32, (SPAN, SPAN), 1)

    @pl.loop(0, heads, step=group)
    def _(base):
        parts = []
        for u in range(group):
            for block in range(2):
                parts.append((slice(block * SPAN, (block + 1) * SPAN), columns(base + u)))
        weights = [jnp.where(causal, matmul(q_ref[rng, cols], k_ref[rng, cols], 1, 1), 0.0).astype(jnp.bfloat16) for rng, cols in parts]
        for (rng, cols), weight in zip(parts, weights):
            intra[rng, cols] = matmul(weight, v_ref[rng, cols], 1, 0)

    def receive(level, c, up):
        hop_arrived(level, c, up)

        @pl.when(has_up if up else has_down)
        def _():
            hop(level, c, up)

    def near():
        @pl.loop(0, chunks)
        def _(c):
            @pl.when(has_up)
            def _():
                receive(z + 1, c, False)

            @pl.when(has_down)
            def _():
                receive(z - 1, c, True)

        @pl.when(has_up)
        def _():
            seconds(z + 1)

        @pl.when(has_down)
        def _():
            seconds(z - 1)

    middle = jnp.logical_and(has_up, has_down)
    pl.when(middle)(near)

    @pl.loop(0, planes)
    def _(level):
        for k in range(1, w):
            m = lax.rem(j + k, w)
            pass_by(t_recv.at[m, level], t_in.at[m, level]).wait()

        @pl.when(has_down)
        def _():
            pass_by(s_recv.at[level], s_in.at[level]).wait()

        state = s_in[level].astype(jnp.float32)
        for m in range(w):
            state = jnp.where(flag[2 * m] > 0, 0.0, state)
            enter[level, m] = state
            state = jnp.where(flag[2 * m + 1] > 0, 0.0, state) + t_in[m, level].astype(jnp.float32)
        s_out[level] = state.astype(jnp.bfloat16)

        @pl.when(has_up)
        def _():
            send(s_out.at[level], s_in.at[level], s_send, s_recv.at[level], me + w).start()

    states(z)
    pl.when(jnp.logical_not(middle))(near)

    @pl.when(has_up)
    def _():
        states(z + 1)

    @pl.when(has_down)
    def _():
        states(z - 1)

    def finish(level, which):
        for i in which:
            for o in range(pieces):
                owner = i * pieces + o

                @pl.when(owner != j)
                def _():
                    pass_by(d_recv.at[level, owner], d_in.at[level, owner]).wait()

        for i in which:
            cols = columns(level * per_level + i)
            entering = d_in[level, pl.ds(i * pieces, pieces), :, 0].reshape(DK, DV)
            second = d_in[level, pl.ds(i * pieces, pieces), :, 1].reshape(DK, DV)
            later = (entering.astype(jnp.float32) + first[level * per_level + i]).astype(jnp.bfloat16)
            at = (entering, jnp.where(second_starts, second, later))
            for block in range(2):
                rng = slice(block * SPAN, (block + 1) * SPAN)
                o = matmul(q_ref[rng, cols], at[block], 1, 0) + intra[rng, cols]
                scale = lax.rsqrt(jnp.mean(o * o, axis=-1, keepdims=True) + epsilon)
                out_ref[rng, cols] = (o * scale).astype(jnp.bfloat16)
        for i in which:
            cols = columns(level * per_level + i)
            pltpu.make_async_copy(out_ref.at[:, cols], out_hbm.at[:, cols], out_sem).start()

    def both(distance, f):
        @pl.when(z + distance < planes)
        def _():
            f(z + distance, False)

        @pl.when(z - distance >= 0)
        def _():
            f(z - distance, True)

    finish(z, range(per_level))

    @pl.loop(2, planes)
    def _(distance):
        @pl.loop(0, chunks)
        def _(c):
            def step(level, up):
                receive(level, c, up)
                make(level, c, False)
                make(level, c, True)
                give(level, (c,))

            both(distance, step)

        both(distance - 1, lambda level, up: finish(level, range(per_level)))

    both(planes - 1, lambda level, up: finish(level, range(per_level)))

    pltpu.make_async_copy(out_ref, out_hbm, out_sem).wait()
    pass_by(t_send, t_out.at[0:w - 1]).wait()
    pass_by(d_send, d_out.at[:, 0:w - 1]).wait()

    @pl.when(has_up)
    def _():
        pass_by(s_send, s_out).wait()

        @pl.loop(0, z + 1)
        def _(level):
            hop_sent(level, True)

    @pl.when(has_down)
    def _():
        @pl.loop(z, planes)
        def _(level):
            hop_sent(level, False)


def solution(mesh):
    n = mesh.shape["seq"]

    def shards(queries, keys, values, prompt_state, lengths, prompt_of):
        tokens, width = queries.shape
        count, rows, _ = prompt_state.shape
        half = jnp.bfloat16
        w = plane_width(n)
        planes = n // w
        chunks = max(1, rows // 32)
        part = rows // chunks
        anywhere = pl.BlockSpec(memory_space=pl.ANY)
        scalar = pl.BlockSpec(memory_space=pltpu.SMEM)
        dma = pltpu.SemaphoreType.DMA
        regular = pltpu.SemaphoreType.REGULAR
        spread = pltpu.VMEM((planes, w, chunks, 2, part, DV), half)
        sums = pltpu.VMEM((w, planes, rows, DV), half)
        chain = pltpu.VMEM((planes, rows, DV), half)
        block = pltpu.VMEM((tokens, width), half)
        return pl.pallas_call(
            functools.partial(kernel, n),
            out_shape=jax.ShapeDtypeStruct((tokens, width), half),
            in_specs=[anywhere] * 4 + [scalar] * 2,
            out_specs=anywhere,
            scratch_shapes=[
                block, block, block,
                pltpu.VMEM((count, rows, DV), half),
                block,
                pltpu.VMEM((tokens, width), jnp.float32),
                pltpu.VMEM((width // DK, DK, DV), jnp.float32),
                pltpu.VMEM((planes, chunks, lengths.shape[0], part, DV), half),
                sums, sums, chain, chain,
                pltpu.VMEM((planes, w, rows, DV), jnp.float32),
                spread, spread,
                pltpu.SMEM((2 * w,), jnp.int32),
                pltpu.SMEM((2 * w,), jnp.int32),
                regular, regular,
                dma((4,)), dma(()), dma((planes, 2)), dma((planes, chunks)), dma(()), dma((w, planes)),
                dma(()), dma((planes,)), dma(()), dma((planes, w)),
            ],
            compiler_params=pltpu.CompilerParams(
                collective_id=0, has_side_effects=True, vmem_limit_bytes=62 << 20),
        )(queries, keys, values, prompt_state, lengths, prompt_of.reshape(-1))

    placed = (
        P(("groups", "seq"), None),
        P(("groups", "seq"), None),
        P(("groups", "seq"), None),
        P("groups", "seq", None),
        P("groups"),
        P("groups", None),
    )
    return jax.shard_map(
        shards, mesh=mesh, in_specs=placed, out_specs=P(("groups", "seq"), None), check_vma=False
    )
```

```python
import functools
import jax
import jax.numpy as jnp
from jax import lax
from jax.experimental import pallas as pl
from jax.experimental.pallas import tpu as pltpu
from jax.sharding import PartitionSpec as P

DK = 128
DV = 128
SPAN = 128
epsilon = 1e-06


def matmul(a, b, ca, cb):
    return lax.dot_general(a, b, (((ca,), (cb,)), ((), ())), preferred_element_type=jnp.float32)


def plane_width(n):
    x = 1
    while (2 * x) ** 3 <= n // 2:
        x *= 2
    return 2 * x


def kernel(n, q_hbm, k_hbm, v_hbm, p_hbm, len_ref, of_ref, out_hbm,
           q_ref, k_ref, v_ref, prompts, out_ref, intra, first, gathered, t_own, t_mate, tc_out, tc_in, s_out, s_in, enter, d_out, d_in, flag, index,
           ready_up, ready_mate, load_sem, out_sem, g_send, g_recv, t_send, t_recv, tc_send, tc_recv, s_send, s_recv, d_send, d_recv):
    me = lax.axis_index("seq")
    w = plane_width(n)
    planes = n // w
    z = me // w
    j = lax.rem(me, w)
    upper = 2 * z >= planes
    chips = w // 2
    x = j // 2
    core = lax.rem(j, 2)
    mate = me + 1 - 2 * core
    heads = k_ref.shape[1] // DK
    rows = prompts.shape[1]
    pieces = DK // rows
    per_level = w // pieces
    _, chunks, responses, part, _ = gathered.shape
    some = responses - 1

    def load(i, src, dst):
        return pltpu.make_async_copy(src, dst, load_sem.at[i])

    loads = [load(0, p_hbm, prompts), load(1, k_hbm, k_ref), load(2, v_hbm, v_ref), load(3, q_hbm, q_ref)]
    for copy in loads:
        copy.start()

    def signal(sem, device):
        pl.semaphore_signal(sem, inc=1, device_id={"seq": device}, device_id_type=pl.DeviceIdType.MESH)

    def send(src, dst, send_sem, recv_sem, target):
        return pltpu.make_async_remote_copy(
            src_ref=src, dst_ref=dst, send_sem=send_sem, recv_sem=recv_sem,
            device_id={"seq": target}, device_id_type=pl.DeviceIdType.MESH)

    def pass_by(sem, ref):
        return pltpu.make_async_copy(ref, ref, sem)

    barrier = pltpu.get_barrier_semaphore()
    has_up = z < planes - 1
    has_down = z > 0

    @pl.when(has_up)
    def _():
        signal(barrier, me + w)

    @pl.loop(j + 1, w)
    def _(m):
        signal(barrier, z * w + m)

    @pl.when(me > 0)
    def _():
        pl.semaphore_wait(barrier, j + jnp.where(has_down, 1, 0))

    @pl.when(has_down)
    def _():
        signal(ready_up, me - w)

    @pl.loop(0, j)
    def _(m):
        signal(ready_mate, z * w + m)

    def hop(level, c, up):
        target = jnp.where(up, me + w, me - w)
        target_upper = 2 * jnp.where(up, z + 1, z - 1) >= planes

        def go(low, count):
            ref = gathered.at[level, c, pl.ds(low, count)]
            send(ref, ref, g_send.at[level, int(up)], g_recv.at[level, c], target).start()

        @pl.when(target_upper != up)
        def _():
            go(0, responses)

        @pl.when(target_upper == up)
        def _():
            go(int(up), some)

    def hop_sent(level, up):
        target_upper = 2 * jnp.where(up, z + 1, z - 1) >= planes

        @pl.when(target_upper != up)
        def _():
            pass_by(g_send.at[level, int(up)], gathered.at[level]).wait()

        @pl.when(target_upper == up)
        def _():
            pass_by(g_send.at[level, int(up)], gathered.at[level, :, pl.ds(int(up), some)]).wait()

    def hop_arrived(level, c, up):
        @pl.when(upper != up)
        def _():
            pass_by(g_recv.at[level, c], gathered.at[level, c]).wait()

        @pl.when(upper == up)
        def _():
            pass_by(g_recv.at[level, c], gathered.at[level, c, pl.ds(int(up), some)]).wait()

    loads[0].wait()
    for r in range(responses):
        gathered[z, :, r] = prompts[of_ref[r]].reshape(chunks, part, DV)

    @pl.when(has_down)
    def _():
        for c in range(chunks):
            hop(z, c, False)

    @pl.loop(0, 2 * w)
    def _(i):
        c = 2 * z * w + i
        start = jnp.int32(0)
        begins = jnp.int32(0)
        which = jnp.int32(-1)
        for r in range(responses):
            begins = begins + jnp.where(start == c, 1, 0)
            which = which + jnp.where(start <= c, 1, 0)
            start = start + len_ref[r]
        flag[i] = begins
        index[i] = which

    @pl.when(z == 0)
    def _():
        s_in[...] = jnp.zeros_like(s_in)

    second_starts = flag[2 * j + 1] > 0
    group = 4

    def columns(h):
        return pl.ds(pl.multiple_of(h * DK, DK), DK)

    loads[1].wait()
    loads[2].wait()

    @pl.loop(0, heads, step=group)
    def _(base):
        for u in range(group):
            h = base + u
            cols = columns(h)
            a = matmul(k_ref[0:SPAN, cols], v_ref[0:SPAN, cols], 0, 0)
            b = matmul(k_ref[SPAN:2 * SPAN, cols], v_ref[SPAN:2 * SPAN, cols], 0, 0)
            first[h] = a
            total = jnp.where(second_starts, b, a + b).astype(jnp.bfloat16)
            for p in range(pieces):
                g = h * pieces + p
                t_own[lax.rem(g, w), g // w] = total[p * rows:(p + 1) * rows]

    @pl.when(has_up)
    def _():
        pl.semaphore_wait(ready_up, 1)
        for c in range(chunks):
            hop(z, c, True)

    @pl.when(j < w - 1)
    def _():
        pl.semaphore_wait(ready_mate, w - 1 - j)

    @pl.loop(0, planes)
    def _(level):
        send(t_own.at[:, level], t_mate.at[:, level], t_send, t_recv.at[level], mate).start()

    low = jnp.where(upper, 1, 0)

    def prompt(level, c, block):
        which = index[block]
        chosen = gathered[level, c, low]
        for r in range(1, some):
            chosen = jnp.where(which == low + r, gathered[level, c, low + r], chosen)
        return chosen

    def make(level, c, second):
        for k in range(w):
            m = lax.rem(j + k, w)
            ref = d_in.at[level, j] if k == 0 else d_out.at[level, m]
            if second:
                ref[c, 1] = prompt(level, c, 2 * m + 1)
            else:
                entering = enter[level, m, c * part:(c + 1) * part] if isinstance(c, int) else enter[level, m, pl.ds(pl.multiple_of(c * part, part), part)]
                ref[c, 0] = (prompt(level, c, 2 * m).astype(jnp.float32) + entering).astype(jnp.bfloat16)

    def give(level, where):
        for k in range(1, w):
            m = lax.rem(j + k, w)
            send(d_out.at[level, m].at[where], d_in.at[level, j].at[where], d_send, d_recv.at[level, j], z * w + m).start()

    def seconds(level):
        for c in range(chunks):
            make(level, c, True)
        give(level, (slice(None), 1))

    def states(level):
        for c in range(chunks):
            make(level, c, False)
        give(level, (slice(None), 0))

    seconds(z)
    late = flag[4 * x + 2] + flag[4 * x + 3] > 0

    @pl.loop(0, planes)
    def _(level):
        pass_by(t_recv.at[level], t_mate.at[:, level]).wait()
        for k in range(chips):
            to = lax.rem(x + k, chips)
            column = 2 * to + core
            own = t_own[column, level].astype(jnp.float32)
            other = t_mate[column, level].astype(jnp.float32)
            total = jnp.where(late, jnp.where(core == 1, own, other), own + other).astype(jnp.bfloat16)
            if k == 0:
                tc_in[x, level] = total
            else:
                tc_out[to, level] = total
                send(tc_out.at[to, level], tc_in.at[x, level], tc_send, tc_recv.at[x, level], z * w + column).start()

    loads[3].wait()
    causal = lax.broadcasted_iota(jnp.int32, (SPAN, SPAN), 0) >= lax.broadcasted_iota(jnp.int32, (SPAN, SPAN), 1)

    @pl.loop(0, heads, step=group)
    def _(base):
        parts = []
        for u in range(group):
            for block in range(2):
                parts.append((slice(block * SPAN, (block + 1) * SPAN), columns(base + u)))
        weights = [jnp.where(causal, matmul(q_ref[rng, cols], k_ref[rng, cols], 1, 1), 0.0).astype(jnp.bfloat16) for rng, cols in parts]
        for (rng, cols), weight in zip(parts, weights):
            intra[rng, cols] = matmul(weight, v_ref[rng, cols], 1, 0)

    def receive(level, c, up):
        hop_arrived(level, c, up)

        @pl.when(has_up if up else has_down)
        def _():
            hop(level, c, up)

    def near():
        @pl.loop(0, chunks)
        def _(c):
            @pl.when(has_up)
            def _():
                receive(z + 1, c, False)

            @pl.when(has_down)
            def _():
                receive(z - 1, c, True)

        @pl.when(has_up)
        def _():
            seconds(z + 1)

        @pl.when(has_down)
        def _():
            seconds(z - 1)

    pl.when(has_down)(near)

    @pl.loop(0, planes)
    def _(level):
        for k in range(1, chips):
            other = lax.rem(x + k, chips)
            pass_by(tc_recv.at[other, level], tc_in.at[other, level]).wait()

        @pl.when(has_down)
        def _():
            pass_by(s_recv.at[level], s_in.at[level]).wait()

        state = s_in[level].astype(jnp.float32)
        for i in range(chips):
            state = jnp.where(flag[4 * i] > 0, 0.0, state)
            enter[level, 2 * i] = state
            inside = flag[4 * i + 1] + flag[4 * i + 2]
            enter[level, 2 * i + 1] = jnp.where(inside > 0, 0.0, state)
            state = jnp.where(inside + flag[4 * i + 3] > 0, 0.0, state) + tc_in[i, level].astype(jnp.float32)
        s_out[level] = state.astype(jnp.bfloat16)

        @pl.when(has_up)
        def _():
            send(s_out.at[level], s_in.at[level], s_send, s_recv.at[level], me + w).start()

    pl.when(z == 0)(near)
    fresh = jnp.logical_and(core == 1, flag[2 * j] == 0)

    def finish(level, which):
        for i in which:
            for o in range(pieces):
                owner = i * pieces + o

                @pl.when(owner != j)
                def _():
                    pass_by(d_recv.at[level, owner], d_in.at[level, owner]).wait()

        for i in which:
            cols = columns(level * per_level + i)
            entering = d_in[level, pl.ds(i * pieces, pieces), :, 0].reshape(DK, DV)
            second = d_in[level, pl.ds(i * pieces, pieces), :, 1].reshape(DK, DV)
            before = t_mate[pl.ds(i * pieces, pieces), level].reshape(DK, DV)
            state = entering.astype(jnp.float32) + jnp.where(fresh, before.astype(jnp.float32), 0.0)
            later = (state + first[level * per_level + i]).astype(jnp.bfloat16)
            at = (state.astype(jnp.bfloat16), jnp.where(second_starts, second, later))
            for block in range(2):
                rng = slice(block * SPAN, (block + 1) * SPAN)
                o = matmul(q_ref[rng, cols], at[block], 1, 0) + intra[rng, cols]
                scale = lax.rsqrt(jnp.mean(o * o, axis=-1, keepdims=True) + epsilon)
                out_ref[rng, cols] = (o * scale).astype(jnp.bfloat16)
        for i in which:
            cols = columns(level * per_level + i)
            pltpu.make_async_copy(out_ref.at[:, cols], out_hbm.at[:, cols], out_sem).start()

    def both(distance, f):
        @pl.when(z + distance < planes)
        def _():
            f(z + distance, False)

        @pl.when(z - distance >= 0)
        def _():
            f(z - distance, True)

    def whole(level):
        finish(level, range(per_level))

    def far(distance, others):
        for c in range(chunks):
            def step(level, up):
                receive(level, c, up)

            both(distance, step)
            for other in others[c:c + 1] if c < chunks - 1 else others[c:]:
                other()

            def pass_on(level, up):
                make(level, c, False)
                make(level, c, True)
                give(level, (c,))

            both(distance, pass_on)

    def above(distance, f):
        def go():
            pl.when(z + distance < planes)(lambda: f(z + distance))
        return go

    def below(distance, f):
        def go():
            pl.when(z - distance >= 0)(lambda: f(z - distance))
        return go

    far(2, [lambda: states(z), above(1, states), below(1, states)])
    far(3, [lambda: whole(z), above(1, whole), below(1, whole)])
    if planes > 4:
        @pl.loop(4, planes)
        def _(distance):
            far(distance, [above(distance - 2, whole), below(distance - 2, whole)])

    for distance in (planes - 2, planes - 1):
        above(distance, whole)()
        below(distance, whole)()

    pltpu.make_async_copy(out_ref, out_hbm, out_sem).wait()
    pass_by(t_send, t_own).wait()
    pass_by(tc_send, tc_out.at[0:chips - 1]).wait()
    pass_by(d_send, d_out.at[:, 0:w - 1]).wait()

    @pl.when(has_up)
    def _():
        pass_by(s_send, s_out).wait()

        @pl.loop(0, z + 1)
        def _(level):
            hop_sent(level, True)

    @pl.when(has_down)
    def _():
        @pl.loop(z, planes)
        def _(level):
            hop_sent(level, False)


def solution(mesh):
    n = mesh.shape["seq"]

    def shards(queries, keys, values, prompt_state, lengths, prompt_of):
        tokens, width = queries.shape
        count, rows, _ = prompt_state.shape
        half = jnp.bfloat16
        w = plane_width(n)
        planes = n // w
        chunks = max(1, rows // 32)
        part = rows // chunks
        anywhere = pl.BlockSpec(memory_space=pl.ANY)
        scalar = pl.BlockSpec(memory_space=pltpu.SMEM)
        dma = pltpu.SemaphoreType.DMA
        regular = pltpu.SemaphoreType.REGULAR
        spread = pltpu.VMEM((planes, w, chunks, 2, part, DV), half)
        sums = pltpu.VMEM((w, planes, rows, DV), half)
        chips = pltpu.VMEM((w // 2, planes, rows, DV), half)
        chain = pltpu.VMEM((planes, rows, DV), half)
        block = pltpu.VMEM((tokens, width), half)
        return pl.pallas_call(
            functools.partial(kernel, n),
            out_shape=jax.ShapeDtypeStruct((tokens, width), half),
            in_specs=[anywhere] * 4 + [scalar] * 2,
            out_specs=anywhere,
            scratch_shapes=[
                block, block, block,
                pltpu.VMEM((count, rows, DV), half),
                block,
                pltpu.VMEM((tokens, width), jnp.float32),
                pltpu.VMEM((width // DK, DK, DV), jnp.float32),
                pltpu.VMEM((planes, chunks, lengths.shape[0], part, DV), half),
                sums, sums, chips, chips, chain, chain,
                pltpu.VMEM((planes, w, rows, DV), jnp.float32),
                spread, spread,
                pltpu.SMEM((2 * w,), jnp.int32),
                pltpu.SMEM((2 * w,), jnp.int32),
                regular, regular,
                dma((4,)), dma(()), dma((planes, 2)), dma((planes, chunks)), dma(()), dma((planes,)),
                dma(()), dma((w // 2, planes)),
                dma(()), dma((planes,)), dma(()), dma((planes, w)),
            ],
            compiler_params=pltpu.CompilerParams(
                collective_id=0, has_side_effects=True, vmem_limit_bytes=62 << 20),
        )(queries, keys, values, prompt_state, lengths, prompt_of.reshape(-1))

    placed = (
        P(("groups", "seq"), None),
        P(("groups", "seq"), None),
        P(("groups", "seq"), None),
        P("groups", "seq", None),
        P("groups"),
        P("groups", None),
    )
    return jax.shard_map(
        shards, mesh=mesh, in_specs=placed, out_specs=P(("groups", "seq"), None), check_vma=False
    )
```

```python
import functools
import jax
import jax.numpy as jnp
from jax import lax
from jax.experimental import pallas as pl
from jax.experimental.pallas import tpu as pltpu
from jax.sharding import PartitionSpec as P

DK = 128
DV = 128
SPAN = 128
epsilon = 1e-06


def matmul(a, b, ca, cb):
    return lax.dot_general(a, b, (((ca,), (cb,)), ((), ())), preferred_element_type=jnp.float32)


def plane_width(n):
    x = 1
    while (2 * x) ** 3 <= n // 2:
        x *= 2
    return 2 * x


def kernel(n, q_hbm, k_hbm, v_hbm, p_hbm, len_ref, of_ref, out_hbm,
           q_ref, k_ref, v_ref, prompts, out_ref, intra, first, gathered, t_own, t_mate, tc_out, tc_in, s_out, s_in, enter, d_out, d_in, flag, index,
           ready_up, ready_mate, load_sem, out_sem, g_send, g_recv, t_send, t_recv, tc_send, tc_recv, s_send, s_recv, d_send, d_recv):
    me = lax.axis_index("seq")
    w = plane_width(n)
    planes = n // w
    z = me // w
    j = lax.rem(me, w)
    upper = 2 * z >= planes
    chips = w // 2
    x = j // 2
    core = lax.rem(j, 2)
    mate = me + 1 - 2 * core
    heads = k_ref.shape[1] // DK
    rows = prompts.shape[1]
    pieces = DK // rows
    per_level = w // pieces
    _, chunks, responses, part, _ = gathered.shape
    some = responses - 1

    def load(i, src, dst):
        return pltpu.make_async_copy(src, dst, load_sem.at[i])

    loads = [load(0, p_hbm, prompts), load(1, k_hbm, k_ref), load(2, v_hbm, v_ref), load(3, q_hbm, q_ref)]
    for copy in loads:
        copy.start()

    def signal(sem, device):
        pl.semaphore_signal(sem, inc=1, device_id={"seq": device}, device_id_type=pl.DeviceIdType.MESH)

    def send(src, dst, send_sem, recv_sem, target):
        return pltpu.make_async_remote_copy(
            src_ref=src, dst_ref=dst, send_sem=send_sem, recv_sem=recv_sem,
            device_id={"seq": target}, device_id_type=pl.DeviceIdType.MESH)

    def pass_by(sem, ref):
        return pltpu.make_async_copy(ref, ref, sem)

    barrier = pltpu.get_barrier_semaphore()
    has_up = z < planes - 1
    has_down = z > 0

    @pl.when(has_up)
    def _():
        signal(barrier, me + w)

    @pl.loop(j + 1, w)
    def _(m):
        signal(barrier, z * w + m)

    @pl.when(me > 0)
    def _():
        pl.semaphore_wait(barrier, j + jnp.where(has_down, 1, 0))

    @pl.when(has_down)
    def _():
        signal(ready_up, me - w)

    @pl.loop(0, j)
    def _(m):
        signal(ready_mate, z * w + m)

    def hop(level, c, up):
        target = jnp.where(up, me + w, me - w)
        target_upper = 2 * jnp.where(up, z + 1, z - 1) >= planes

        def go(low, count):
            ref = gathered.at[level, c, pl.ds(low, count)]
            send(ref, ref, g_send.at[level, int(up)], g_recv.at[level, c], target).start()

        @pl.when(target_upper != up)
        def _():
            go(0, responses)

        @pl.when(target_upper == up)
        def _():
            go(int(up), some)

    def hop_sent(level, up):
        target_upper = 2 * jnp.where(up, z + 1, z - 1) >= planes

        @pl.when(target_upper != up)
        def _():
            pass_by(g_send.at[level, int(up)], gathered.at[level]).wait()

        @pl.when(target_upper == up)
        def _():
            pass_by(g_send.at[level, int(up)], gathered.at[level, :, pl.ds(int(up), some)]).wait()

    def hop_arrived(level, c, up):
        @pl.when(upper != up)
        def _():
            pass_by(g_recv.at[level, c], gathered.at[level, c]).wait()

        @pl.when(upper == up)
        def _():
            pass_by(g_recv.at[level, c], gathered.at[level, c, pl.ds(int(up), some)]).wait()

    loads[0].wait()
    for r in range(responses):
        gathered[z, :, r] = prompts[of_ref[r]].reshape(chunks, part, DV)

    @pl.when(has_down)
    def _():
        for c in range(chunks):
            hop(z, c, False)

    @pl.loop(0, 2 * w)
    def _(i):
        c = 2 * z * w + i
        start = jnp.int32(0)
        begins = jnp.int32(0)
        which = jnp.int32(-1)
        for r in range(responses):
            begins = begins + jnp.where(start == c, 1, 0)
            which = which + jnp.where(start <= c, 1, 0)
            start = start + len_ref[r]
        flag[i] = begins
        index[i] = which

    @pl.when(z == 0)
    def _():
        s_in[...] = jnp.zeros_like(s_in)

    second_starts = flag[2 * j + 1] > 0
    def columns(h):
        return pl.ds(pl.multiple_of(h * DK, DK), DK)

    low = jnp.where(upper, 1, 0)

    def prompt(level, c, block):
        which = index[block]
        chosen = gathered[level, c, low]
        for r in range(1, some):
            chosen = jnp.where(which == low + r, gathered[level, c, low + r], chosen)
        return chosen

    def make(level, c, second):
        for k in range(w):
            m = lax.rem(j + k, w)
            ref = d_in.at[level, j] if k == 0 else d_out.at[level, m]
            if second:
                ref[c, 1] = prompt(level, c, 2 * m + 1)
            else:
                entering = enter[level, m, c * part:(c + 1) * part] if isinstance(c, int) else enter[level, m, pl.ds(pl.multiple_of(c * part, part), part)]
                ref[c, 0] = (prompt(level, c, 2 * m).astype(jnp.float32) + entering).astype(jnp.bfloat16)

    def give(level, where):
        for k in range(1, w):
            m = lax.rem(j + k, w)
            send(d_out.at[level, m].at[where], d_in.at[level, j].at[where], d_send, d_recv.at[level, j], z * w + m).start()

    def seconds(level):
        for c in range(chunks):
            make(level, c, True)
        give(level, (slice(None), 1))

    def states(level):
        for c in range(chunks):
            make(level, c, False)
        give(level, (slice(None), 0))

    @pl.when(j < w - 1)
    def _():
        pl.semaphore_wait(ready_mate, w - 1 - j)

    seconds(z)

    @pl.when(has_up)
    def _():
        pl.semaphore_wait(ready_up, 1)
        for c in range(chunks):
            hop(z, c, True)

    loads[1].wait()
    loads[2].wait()

    def share(level, half, number):
        send(t_own.at[half, :, level], t_mate.at[half, :, level], t_send.at[number], t_recv.at[number, level], mate).start()

    @pl.loop(0, planes)
    def _(level):
        for i in range(per_level):
            h = level * per_level + i
            cols = columns(h)
            a = matmul(k_ref[0:SPAN, cols], v_ref[0:SPAN, cols], 0, 0)
            b = matmul(k_ref[SPAN:2 * SPAN, cols], v_ref[SPAN:2 * SPAN, cols], 0, 0)
            first[h] = a
            total = jnp.where(second_starts, b, a + b).astype(jnp.bfloat16)
            for p in range(pieces):
                column = i * pieces + p
                t_own[column % 2, column // 2, level] = total[p * rows:(p + 1) * rows]
        share(level, 1 - core, 0)

    late = flag[4 * x + 2] + flag[4 * x + 3] > 0

    @pl.loop(0, planes)
    def _(level):
        pass_by(t_recv.at[0, level], t_mate.at[core, :, level]).wait()
        for k in range(chips):
            to = lax.rem(x + k, chips)
            column = 2 * to + core
            own = t_own[core, to, level].astype(jnp.float32)
            other = t_mate[core, to, level].astype(jnp.float32)
            total = jnp.where(late, jnp.where(core == 1, own, other), own + other).astype(jnp.bfloat16)
            if k == 0:
                tc_in[x, level] = total
            else:
                tc_out[to, level] = total
                send(tc_out.at[to, level], tc_in.at[x, level], tc_send, tc_recv.at[x, level], z * w + column).start()

    @pl.when(core == 0)
    def _():
        @pl.loop(0, planes)
        def _(level):
            share(level, 0, 1)

    loads[3].wait()
    causal = lax.broadcasted_iota(jnp.int32, (SPAN, SPAN), 0) >= lax.broadcasted_iota(jnp.int32, (SPAN, SPAN), 1)

    group = 4

    @pl.loop(0, heads, step=group)
    def _(base):
        parts = []
        for u in range(group):
            for block in range(2):
                parts.append((slice(block * SPAN, (block + 1) * SPAN), columns(base + u)))
        weights = [jnp.where(causal, matmul(q_ref[rng, cols], k_ref[rng, cols], 1, 1), 0.0).astype(jnp.bfloat16) for rng, cols in parts]
        for (rng, cols), weight in zip(parts, weights):
            intra[rng, cols] = matmul(weight, v_ref[rng, cols], 1, 0)

    def receive(level, c, up):
        hop_arrived(level, c, up)

        @pl.when(has_up if up else has_down)
        def _():
            hop(level, c, up)

    def near(level, up):
        @pl.loop(0, chunks)
        def _(c):
            receive(level, c, up)

        seconds(level)

    def from_above():
        near(z + 1, False)

    def from_below():
        near(z - 1, True)

    pl.when(jnp.logical_and(has_up, has_down))(from_above)
    pl.when(upper)(from_below)

    @pl.loop(0, planes)
    def _(level):
        for k in range(1, chips):
            other = lax.rem(x + k, chips)
            pass_by(tc_recv.at[other, level], tc_in.at[other, level]).wait()

        @pl.when(has_down)
        def _():
            pass_by(s_recv.at[level], s_in.at[level]).wait()

        state = s_in[level].astype(jnp.float32)
        for i in range(chips):
            state = jnp.where(flag[4 * i] > 0, 0.0, state)
            enter[level, 2 * i] = state
            inside = flag[4 * i + 1] + flag[4 * i + 2]
            enter[level, 2 * i + 1] = jnp.where(inside > 0, 0.0, state)
            state = jnp.where(inside + flag[4 * i + 3] > 0, 0.0, state) + tc_in[i, level].astype(jnp.float32)
        s_out[level] = state.astype(jnp.bfloat16)

        @pl.when(has_up)
        def _():
            send(s_out.at[level], s_in.at[level], s_send, s_recv.at[level], me + w).start()

    pl.when(z == 0)(from_above)
    pl.when(jnp.logical_and(has_down, jnp.logical_not(upper)))(from_below)
    fresh = jnp.logical_and(core == 1, flag[2 * j] == 0)

    def finish(level, which):
        @pl.when(core == 1)
        def _():
            pass_by(t_recv.at[1, level], t_mate.at[0, :, level]).wait()

        for i in which:
            for o in range(pieces):
                owner = i * pieces + o

                @pl.when(owner != j)
                def _():
                    pass_by(d_recv.at[level, owner], d_in.at[level, owner]).wait()

        for i in which:
            cols = columns(level * per_level + i)
            entering = d_in[level, pl.ds(i * pieces, pieces), :, 0].reshape(DK, DV)
            second = d_in[level, pl.ds(i * pieces, pieces), :, 1].reshape(DK, DV)
            before = jnp.concatenate([t_mate[o % 2, o // 2, level] for o in range(i * pieces, (i + 1) * pieces)], axis=0)
            state = entering.astype(jnp.float32) + jnp.where(fresh, before.astype(jnp.float32), 0.0)
            later = (state + first[level * per_level + i]).astype(jnp.bfloat16)
            at = (state.astype(jnp.bfloat16), jnp.where(second_starts, second, later))
            for block in range(2):
                rng = slice(block * SPAN, (block + 1) * SPAN)
                o = matmul(q_ref[rng, cols], at[block], 1, 0) + intra[rng, cols]
                scale = lax.rsqrt(jnp.mean(o * o, axis=-1, keepdims=True) + epsilon)
                out_ref[rng, cols] = (o * scale).astype(jnp.bfloat16)
        for i in which:
            cols = columns(level * per_level + i)
            pltpu.make_async_copy(out_ref.at[:, cols], out_hbm.at[:, cols], out_sem).start()

    def both(distance, f):
        @pl.when(z + distance < planes)
        def _():
            f(z + distance, False)

        @pl.when(z - distance >= 0)
        def _():
            f(z - distance, True)

    def whole(level):
        finish(level, range(per_level))

    def far(distance, others):
        for c in range(chunks):
            def step(level, up):
                receive(level, c, up)

            both(distance, step)
            for other in others[c:c + 1] if c < chunks - 1 else others[c:]:
                other()

            def pass_on(level, up):
                make(level, c, False)
                make(level, c, True)
                give(level, (c,))

            both(distance, pass_on)

    def above(distance, f):
        def go():
            pl.when(z + distance < planes)(lambda: f(z + distance))
        return go

    def below(distance, f):
        def go():
            pl.when(z - distance >= 0)(lambda: f(z - distance))
        return go

    far(2, [lambda: states(z), above(1, states), below(1, states)])
    far(3, [lambda: whole(z), above(1, whole), below(1, whole)])
    if planes > 4:
        @pl.loop(4, planes)
        def _(distance):
            far(distance, [above(distance - 2, whole), below(distance - 2, whole)])

    for distance in (planes - 2, planes - 1):
        above(distance, whole)()
        below(distance, whole)()

    pltpu.make_async_copy(out_ref, out_hbm, out_sem).wait()
    pass_by(t_send.at[0], t_own.at[0]).wait()

    @pl.when(core == 0)
    def _():
        pass_by(t_send.at[1], t_own.at[0]).wait()

    pass_by(tc_send, tc_out.at[0:chips - 1]).wait()
    pass_by(d_send, d_out.at[:, 0:w - 1]).wait()

    @pl.when(has_up)
    def _():
        pass_by(s_send, s_out).wait()

        @pl.loop(0, z + 1)
        def _(level):
            hop_sent(level, True)

    @pl.when(has_down)
    def _():
        @pl.loop(z, planes)
        def _(level):
            hop_sent(level, False)


def solution(mesh):
    n = mesh.shape["seq"]

    def shards(queries, keys, values, prompt_state, lengths, prompt_of):
        tokens, width = queries.shape
        count, rows, _ = prompt_state.shape
        half = jnp.bfloat16
        w = plane_width(n)
        planes = n // w
        chunks = max(1, rows // 32)
        part = rows // chunks
        anywhere = pl.BlockSpec(memory_space=pl.ANY)
        scalar = pl.BlockSpec(memory_space=pltpu.SMEM)
        dma = pltpu.SemaphoreType.DMA
        regular = pltpu.SemaphoreType.REGULAR
        spread = pltpu.VMEM((planes, w, chunks, 2, part, DV), half)
        sums = pltpu.VMEM((2, w // 2, planes, rows, DV), half)
        chips = pltpu.VMEM((w // 2, planes, rows, DV), half)
        chain = pltpu.VMEM((planes, rows, DV), half)
        block = pltpu.VMEM((tokens, width), half)
        return pl.pallas_call(
            functools.partial(kernel, n),
            out_shape=jax.ShapeDtypeStruct((tokens, width), half),
            in_specs=[anywhere] * 4 + [scalar] * 2,
            out_specs=anywhere,
            scratch_shapes=[
                block, block, block,
                pltpu.VMEM((count, rows, DV), half),
                block,
                pltpu.VMEM((tokens, width), jnp.float32),
                pltpu.VMEM((width // DK, DK, DV), jnp.float32),
                pltpu.VMEM((planes, chunks, lengths.shape[0], part, DV), half),
                sums, sums, chips, chips, chain, chain,
                pltpu.VMEM((planes, w, rows, DV), jnp.float32),
                spread, spread,
                pltpu.SMEM((2 * w,), jnp.int32),
                pltpu.SMEM((2 * w,), jnp.int32),
                regular, regular,
                dma((4,)), dma(()), dma((planes, 2)), dma((planes, chunks)), dma((2,)), dma((2, planes)),
                dma(()), dma((w // 2, planes)),
                dma(()), dma((planes,)), dma(()), dma((planes, w)),
            ],
            compiler_params=pltpu.CompilerParams(
                collective_id=0, has_side_effects=True, vmem_limit_bytes=62 << 20),
        )(queries, keys, values, prompt_state, lengths, prompt_of.reshape(-1))

    placed = (
        P(("groups", "seq"), None),
        P(("groups", "seq"), None),
        P(("groups", "seq"), None),
        P("groups", "seq", None),
        P("groups"),
        P("groups", None),
    )
    return jax.shard_map(
        shards, mesh=mesh, in_specs=placed, out_specs=P(("groups", "seq"), None), check_vma=False
    )
```

```python
import functools
import jax
import jax.numpy as jnp
from jax import lax
from jax.experimental import pallas as pl
from jax.experimental.pallas import tpu as pltpu
from jax.sharding import PartitionSpec as P

DK = 128
DV = 128
SPAN = 128
epsilon = 1e-06


def matmul(a, b, ca, cb):
    return lax.dot_general(a, b, (((ca,), (cb,)), ((), ())), preferred_element_type=jnp.float32)


def plane_width(n):
    x = 1
    while (2 * x) ** 3 <= n // 2:
        x *= 2
    return 2 * x


def kernel(n, q_hbm, k_hbm, v_hbm, p_hbm, len_ref, of_ref, out_hbm,
           q_ref, k_ref, v_ref, prompts, out_ref, intra, first, gathered, t_own, t_mate, tc_out, tc_in, s_out, s_in, e_out, e_in, d_out, d_in, flag, index,
           ready_up, ready_mate, load_sem, out_sem, g_send, g_recv, t_send, t_recv, tc_send, tc_recv, s_send, s_recv, e_send, e_recv, d_send, d_recv):
    me = lax.axis_index("seq")
    w = plane_width(n)
    planes = n // w
    z = me // w
    j = lax.rem(me, w)
    upper = 2 * z >= planes
    chips = w // 2
    x = j // 2
    core = lax.rem(j, 2)
    mate = me + 1 - 2 * core
    heads = k_ref.shape[1] // DK
    rows = prompts.shape[1]
    pieces = DK // rows
    per_level = w // pieces
    _, chunks, responses, part, _ = gathered.shape
    some = responses - 1

    def load(i, src, dst):
        return pltpu.make_async_copy(src, dst, load_sem.at[i])

    loads = [load(0, p_hbm, prompts), load(1, k_hbm, k_ref), load(2, v_hbm, v_ref), load(3, q_hbm, q_ref)]
    for copy in loads:
        copy.start()

    def signal(sem, device):
        pl.semaphore_signal(sem, inc=1, device_id={"seq": device}, device_id_type=pl.DeviceIdType.MESH)

    def send(src, dst, send_sem, recv_sem, target):
        return pltpu.make_async_remote_copy(
            src_ref=src, dst_ref=dst, send_sem=send_sem, recv_sem=recv_sem,
            device_id={"seq": target}, device_id_type=pl.DeviceIdType.MESH)

    def pass_by(sem, ref):
        return pltpu.make_async_copy(ref, ref, sem)

    barrier = pltpu.get_barrier_semaphore()
    has_up = z < planes - 1
    has_down = z > 0

    @pl.when(has_up)
    def _():
        signal(barrier, me + w)

    @pl.loop(j + 1, w)
    def _(m):
        signal(barrier, z * w + m)

    @pl.when(me > 0)
    def _():
        pl.semaphore_wait(barrier, j + jnp.where(has_down, 1, 0))

    @pl.when(has_down)
    def _():
        signal(ready_up, me - w)

    @pl.loop(0, j)
    def _(m):
        signal(ready_mate, z * w + m)

    def held(plane, up, f):
        if up:
            last = plane == planes - 1
            pl.when(2 * plane < planes)(lambda: f(0, responses))
            pl.when(jnp.logical_and(2 * plane >= planes, jnp.logical_not(last)))(lambda: f(1, responses - 1))
            pl.when(last)(lambda: f(2, responses - 2))
        else:
            pl.when(2 * plane < planes)(lambda: f(0, responses - 1))
            pl.when(2 * plane >= planes)(lambda: f(0, responses))

    def hop(level, c, up):
        def go(low, count):
            ref = gathered.at[level, c, pl.ds(low, count)]
            send(ref, ref, g_send.at[level, int(up)], g_recv.at[level, c], me + w if up else me - w).start()

        held(z + 1 if up else z - 1, up, go)

    def hop_sent(level, up):
        held(z + 1 if up else z - 1, up, lambda low, count: pass_by(g_send.at[level, int(up)], gathered.at[level, :, pl.ds(low, count)]).wait())

    def hop_arrived(level, c, up):
        held(z, up, lambda low, count: pass_by(g_recv.at[level, c], gathered.at[level, c, pl.ds(low, count)]).wait())

    loads[0].wait()
    for r in range(responses):
        gathered[z, :, r] = prompts[of_ref[r]].reshape(chunks, part, DV)

    @pl.when(has_down)
    def _():
        for c in range(chunks):
            hop(z, c, False)

    last = z == planes - 1

    @pl.loop(0, 2 * w + 1)
    def _(i):
        c = 2 * z * w + i
        start = jnp.int32(0)
        begins = jnp.int32(0)
        which = jnp.int32(-1)
        for r in range(responses):
            begins = begins + jnp.where(start == c, 1, 0)
            which = which + jnp.where(start <= c, 1, 0)
            start = start + len_ref[r]
        flag[i] = begins
        index[i] = which

    started = jnp.where(last, index[0] + jnp.where(flag[0] > 0, 0, 1), 0)

    @pl.when(z == 0)
    def _():
        s_in[...] = jnp.zeros_like(s_in)

    second_starts = flag[2 * j + 1] > 0

    def columns(h):
        return pl.ds(pl.multiple_of(h * DK, DK), DK)

    low = jnp.where(last, 2, jnp.where(upper, 1, 0))

    def prompt(level, c, block, floor):
        which = index[block]
        chosen = jnp.zeros((part, DV), jnp.bfloat16)
        for i in range(some):
            r = jnp.minimum(low + i, responses - 1)
            chosen = jnp.where(jnp.logical_and(which == r, which >= floor), gathered[level, c, r], chosen)
        return chosen

    def make(level, c):
        for k in range(w):
            m = lax.rem(j + k, w)
            ref = d_in.at[level, j] if k == 0 else d_out.at[level, m]
            for block in range(2):
                ref[c, block] = prompt(level, c, 2 * m + block, started)

    def give(level, c):
        for k in range(1, w):
            m = lax.rem(j + k, w)
            send(d_out.at[level, m, c], d_in.at[level, j, c], d_send, d_recv.at[level, j], z * w + m).start()

    @pl.when(j < w - 1)
    def _():
        pl.semaphore_wait(ready_mate, w - 1 - j)

    loads[1].wait()
    loads[2].wait()

    def share(level, half, number):
        send(t_own.at[half, :, level], t_mate.at[half, :, level], t_send.at[number], t_recv.at[number, level], mate).start()

    @pl.loop(0, planes)
    def _(level):
        for i in range(per_level):
            h = level * per_level + i
            cols = columns(h)
            a = matmul(k_ref[0:SPAN, cols], v_ref[0:SPAN, cols], 0, 0)
            b = matmul(k_ref[SPAN:2 * SPAN, cols], v_ref[SPAN:2 * SPAN, cols], 0, 0)
            first[h] = a
            total = jnp.where(second_starts, b, a + b).astype(jnp.bfloat16)
            for p in range(pieces):
                column = i * pieces + p
                t_own[column % 2, column // 2, level] = total[p * rows:(p + 1) * rows]
        share(level, 1 - core, 0)

    @pl.when(has_up)
    def _():
        pl.semaphore_wait(ready_up, 1)
        for c in range(chunks):
            hop(z, c, True)

    late = flag[4 * x + 2] + flag[4 * x + 3] > 0

    @pl.loop(0, planes)
    def _(level):
        pass_by(t_recv.at[0, level], t_mate.at[core, :, level]).wait()
        for k in range(chips):
            to = lax.rem(x + k, chips)
            column = 2 * to + core
            own = t_own[core, to, level].astype(jnp.float32)
            other = t_mate[core, to, level].astype(jnp.float32)
            total = jnp.where(late, jnp.where(core == 1, own, other), own + other).astype(jnp.bfloat16)
            if k == 0:
                tc_in[x, level] = total
            else:
                tc_out[to, level] = total
                send(tc_out.at[to, level], tc_in.at[x, level], tc_send, tc_recv.at[x, level], z * w + column).start()

    for c in range(chunks):
        make(z, c)
        give(z, c)

    @pl.when(core == 0)
    def _():
        @pl.loop(0, planes)
        def _(level):
            share(level, 0, 1)

    loads[3].wait()
    causal = lax.broadcasted_iota(jnp.int32, (SPAN, SPAN), 0) >= lax.broadcasted_iota(jnp.int32, (SPAN, SPAN), 1)

    group = 4

    @pl.loop(0, heads, step=group)
    def _(base):
        parts = []
        for u in range(group):
            for block in range(2):
                parts.append((slice(block * SPAN, (block + 1) * SPAN), columns(base + u)))
        weights = [jnp.where(causal, matmul(q_ref[rng, cols], k_ref[rng, cols], 1, 1), 0.0).astype(jnp.bfloat16) for rng, cols in parts]
        for (rng, cols), weight in zip(parts, weights):
            intra[rng, cols] = matmul(weight, v_ref[rng, cols], 1, 0)

    def receive(level, c, up):
        hop_arrived(level, c, up)

        @pl.when(has_up if up else has_down)
        def _():
            hop(level, c, up)

    def both(distance, f):
        @pl.when(z + distance < planes)
        def _():
            f(z + distance, False)

        @pl.when(z - distance >= 0)
        def _():
            f(z - distance, True)

    def scan(level):
        for k in range(1, chips):
            other = lax.rem(x + k, chips)
            pass_by(tc_recv.at[other, level], tc_in.at[other, level]).wait()

        @pl.when(has_down)
        def _():
            pass_by(s_recv.at[level], s_in.at[level]).wait()

        state = s_in[level].astype(jnp.float32)
        for i in range(chips):
            state = jnp.where(flag[4 * i] > 0, 0.0, state)
            e_out[i, level] = state.astype(jnp.bfloat16)
            inside = flag[4 * i + 1] + flag[4 * i + 2] + flag[4 * i + 3]
            state = jnp.where(inside > 0, 0.0, state) + tc_in[i, level].astype(jnp.float32)

        @pl.when(z != planes - 2)
        def _():
            s_out[level] = state.astype(jnp.bfloat16)

        @pl.when(z == planes - 2)
        def _():
            for c in range(chunks):
                rng = slice(c * part, (c + 1) * part)
                s_out[level, rng] = (state[rng] + prompt(level, c, 2 * w, 0).astype(jnp.float32)).astype(jnp.bfloat16)

        @pl.when(has_up)
        def _():
            send(s_out.at[level], s_in.at[level], s_send, s_recv.at[level], me + w).start()

        for k in range(1, chips):
            to = lax.rem(x + k, chips)
            send(e_out.at[to, level], e_in.at[level, j], e_send.at[1], e_recv.at[level, j], z * w + 2 * to + core).start()
        e_in[level, j] = e_out[x, level]
        send(e_in.at[level, j], e_in.at[level, j], e_send.at[0], e_recv.at[level, j], mate).start()

    def relay(level):
        for k in range(1, chips):
            column = 2 * lax.rem(x + k, chips) + core
            pass_by(e_recv.at[level, column], e_in.at[level, column]).wait()
            send(e_in.at[level, column], e_in.at[level, column], e_send.at[2], e_recv.at[level, column], mate).start()

    def step(distance, c):
        both(distance, lambda level, up: receive(level, c, up))

        def pass_on(level, up):
            make(level, c)
            give(level, c)

        both(distance, pass_on)

    share_of = planes // chunks

    def some_levels(c, f):
        for i in range(share_of):
            f(c * share_of + i)

    def back(i):
        scan(planes - 1 - i)

    def steps(distance, before=None, after=None):
        @pl.loop(0, chunks)
        def _(c):
            if before is not None:
                pl.when(before(c))(lambda: some_levels(c, back))
            step(distance, c)
            if after is not None:
                pl.when(after(c))(lambda: some_levels(c, back))

    if planes == 4:
        steps(1, after=lambda c: z == 0)
        steps(2, before=lambda c: z == 1, after=lambda c: z == 2)
    else:
        steps(1, after=lambda c: z == 0)
        steps(2, after=lambda c: jnp.logical_and(z > 0, z < planes - 2))

        @pl.loop(3, planes - 2)
        def _(distance):
            steps(distance)

        steps(planes - 2, after=lambda c: z == planes - 2)

    @pl.when(z == 0)
    def _():
        pl.loop(0, planes)(lambda i: relay(planes - 1 - i))

    steps(planes - 1, before=lambda c: jnp.logical_and(last, c < chunks - 1), after=lambda c: jnp.logical_and(last, c == chunks - 1))

    fresh = jnp.logical_and(core == 1, flag[2 * j] == 0)
    open_end = jnp.logical_or(core == 0, flag[4 * x + 1] + flag[4 * x + 2] == 0)

    def finish(level, which):
        @pl.when(core == 1)
        def _():
            pass_by(t_recv.at[1, level], t_mate.at[0, :, level]).wait()

        for i in which:
            for o in range(i * pieces, (i + 1) * pieces):
                @pl.when(core != o % 2)
                def _():
                    pass_by(e_recv.at[level, o], e_in.at[level, o]).wait()

        for i in which:
            for o in range(pieces):
                owner = i * pieces + o

                @pl.when(owner != j)
                def _():
                    pass_by(d_recv.at[level, owner], d_in.at[level, owner]).wait()

        for i in which:
            cols = columns(level * per_level + i)
            entering = d_in[level, pl.ds(i * pieces, pieces), :, 0].reshape(DK, DV)
            second = d_in[level, pl.ds(i * pieces, pieces), :, 1].reshape(DK, DV)
            before = jnp.concatenate([t_mate[o % 2, o // 2, level] for o in range(i * pieces, (i + 1) * pieces)], axis=0)
            summed = e_in[level, pl.ds(i * pieces, pieces)].reshape(DK, DV).astype(jnp.float32)
            state = entering.astype(jnp.float32) + jnp.where(open_end, summed, 0.0) + jnp.where(fresh, before.astype(jnp.float32), 0.0)
            later = (state + first[level * per_level + i]).astype(jnp.bfloat16)
            at = (state.astype(jnp.bfloat16), jnp.where(second_starts, second, later))
            for block in range(2):
                rng = slice(block * SPAN, (block + 1) * SPAN)
                o = matmul(q_ref[rng, cols], at[block], 1, 0) + intra[rng, cols]
                scale = lax.rsqrt(jnp.mean(o * o, axis=-1, keepdims=True) + epsilon)
                out_ref[rng, cols] = (o * scale).astype(jnp.bfloat16)
        for i in which:
            cols = columns(level * per_level + i)
            pltpu.make_async_copy(out_ref.at[:, cols], out_hbm.at[:, cols], out_sem).start()

    @pl.when(z == 0)
    def _():
        @pl.loop(0, planes)
        def _(level):
            finish(level, range(per_level))

    @pl.when(has_down)
    def _():
        ahead = 2

        @pl.loop(0, planes + ahead)
        def _(i):
            pl.when(i < planes)(lambda: relay(planes - 1 - i))
            pl.when(i >= ahead)(lambda: finish(planes - 1 + ahead - i, range(per_level)))

    pltpu.make_async_copy(out_ref, out_hbm, out_sem).wait()
    pass_by(t_send.at[0], t_own.at[0]).wait()

    @pl.when(core == 0)
    def _():
        pass_by(t_send.at[1], t_own.at[0]).wait()

    pass_by(tc_send, tc_out.at[0:chips - 1]).wait()
    pass_by(e_send.at[0], s_out).wait()
    pass_by(e_send.at[1], e_out.at[0:chips - 1]).wait()
    pass_by(e_send.at[2], e_out.at[0:chips - 1]).wait()
    pass_by(d_send, d_out.at[:, 0:w - 1]).wait()

    @pl.when(has_up)
    def _():
        pass_by(s_send, s_out).wait()

        @pl.loop(0, z + 1)
        def _(level):
            hop_sent(level, True)

    @pl.when(has_down)
    def _():
        @pl.loop(z, planes)
        def _(level):
            hop_sent(level, False)


def solution(mesh):
    n = mesh.shape["seq"]

    def shards(queries, keys, values, prompt_state, lengths, prompt_of):
        tokens, width = queries.shape
        count, rows, _ = prompt_state.shape
        half = jnp.bfloat16
        w = plane_width(n)
        planes = n // w
        chunks = max(1, rows // 32)
        part = rows // chunks
        anywhere = pl.BlockSpec(memory_space=pl.ANY)
        scalar = pl.BlockSpec(memory_space=pltpu.SMEM)
        dma = pltpu.SemaphoreType.DMA
        regular = pltpu.SemaphoreType.REGULAR
        spread = pltpu.VMEM((planes, w, chunks, 2, part, DV), half)
        sums = pltpu.VMEM((2, w // 2, planes, rows, DV), half)
        chips = pltpu.VMEM((w // 2, planes, rows, DV), half)
        chain = pltpu.VMEM((planes, rows, DV), half)
        block = pltpu.VMEM((tokens, width), half)
        return pl.pallas_call(
            functools.partial(kernel, n),
            out_shape=jax.ShapeDtypeStruct((tokens, width), half),
            in_specs=[anywhere] * 4 + [scalar] * 2,
            out_specs=anywhere,
            scratch_shapes=[
                block, block, block,
                pltpu.VMEM((count, rows, DV), half),
                block,
                pltpu.VMEM((tokens, width), jnp.float32),
                pltpu.VMEM((width // DK, DK, DV), jnp.float32),
                pltpu.VMEM((planes, chunks, lengths.shape[0], part, DV), half),
                sums, sums, chips, chips, chain, chain,
                chips, pltpu.VMEM((planes, w, rows, DV), half),
                spread, spread,
                pltpu.SMEM((2 * w + 1,), jnp.int32),
                pltpu.SMEM((2 * w + 1,), jnp.int32),
                regular, regular,
                dma((4,)), dma(()), dma((planes, 2)), dma((planes, chunks)), dma((2,)), dma((2, planes)),
                dma(()), dma((w // 2, planes)),
                dma(()), dma((planes,)), dma((3,)), dma((planes, w)), dma(()), dma((planes, w)),
            ],
            compiler_params=pltpu.CompilerParams(
                collective_id=0, has_side_effects=True, vmem_limit_bytes=62 << 20),
        )(queries, keys, values, prompt_state, lengths, prompt_of.reshape(-1))

    placed = (
        P(("groups", "seq"), None),
        P(("groups", "seq"), None),
        P(("groups", "seq"), None),
        P("groups", "seq", None),
        P("groups"),
        P("groups", None),
    )
    return jax.shard_map(
        shards, mesh=mesh, in_specs=placed, out_specs=P(("groups", "seq"), None), check_vma=False
    )
```

```python
import functools
import jax
import jax.numpy as jnp
from jax import lax
from jax.experimental import pallas as pl
from jax.experimental.pallas import tpu as pltpu
from jax.sharding import PartitionSpec as P

DK = 128
DV = 128
SPAN = 128
epsilon = 1e-06


def matmul(a, b, ca, cb):
    return lax.dot_general(a, b, (((ca,), (cb,)), ((), ())), preferred_element_type=jnp.float32)


def plane_width(n):
    x = 1
    while (2 * x) ** 3 <= n // 2:
        x *= 2
    return 2 * x


def kernel(n, q_hbm, k_hbm, v_hbm, p_hbm, len_ref, of_ref, out_ref,
           q_ref, k_ref, v_ref, prompts, intra, first, gathered, t_own, t_mate, tc_out, tc_in, s_out, s_in, e_out, e_in, d_out, d_in, flag, index,
           ready_up, ready_mate, load_sem, g_send, g_recv, t_send, t_recv, tc_send, tc_recv, s_send, s_recv, e_send, e_recv, d_send, d_recv):
    me = lax.axis_index("seq")
    w = plane_width(n)
    planes = n // w
    z = me // w
    j = lax.rem(me, w)
    upper = 2 * z >= planes
    chips = w // 2
    x = j // 2
    core = lax.rem(j, 2)
    mate = me + 1 - 2 * core
    heads = k_ref.shape[1] // DK
    rows = prompts.shape[1]
    pieces = DK // rows
    per_level = w // pieces
    _, chunks, responses, part, _ = gathered.shape
    some = responses - 1

    def load(i, src, dst):
        return pltpu.make_async_copy(src, dst, load_sem.at[i])

    loads = [load(0, p_hbm, prompts), load(1, k_hbm, k_ref), load(2, v_hbm, v_ref), load(3, q_hbm, q_ref)]
    for copy in loads:
        copy.start()

    def signal(sem, device):
        pl.semaphore_signal(sem, inc=1, device_id={"seq": device}, device_id_type=pl.DeviceIdType.MESH)

    def send(src, dst, send_sem, recv_sem, target):
        return pltpu.make_async_remote_copy(
            src_ref=src, dst_ref=dst, send_sem=send_sem, recv_sem=recv_sem,
            device_id={"seq": target}, device_id_type=pl.DeviceIdType.MESH)

    def pass_by(sem, ref):
        return pltpu.make_async_copy(ref, ref, sem)

    barrier = pltpu.get_barrier_semaphore()
    has_up = z < planes - 1
    has_down = z > 0

    @pl.when(has_up)
    def _():
        signal(barrier, me + w)

    @pl.loop(j + 1, w)
    def _(m):
        signal(barrier, z * w + m)

    @pl.when(me > 0)
    def _():
        pl.semaphore_wait(barrier, j + jnp.where(has_down, 1, 0))

    @pl.when(has_down)
    def _():
        signal(ready_up, me - w)

    @pl.loop(0, j)
    def _(m):
        signal(ready_mate, z * w + m)

    def held(plane, up, f):
        if up:
            last = plane == planes - 1
            pl.when(2 * plane < planes)(lambda: f(0, responses))
            pl.when(jnp.logical_and(2 * plane >= planes, jnp.logical_not(last)))(lambda: f(1, responses - 1))
            pl.when(last)(lambda: f(2, responses - 2))
        else:
            pl.when(2 * plane < planes)(lambda: f(0, responses - 1))
            pl.when(2 * plane >= planes)(lambda: f(0, responses))

    def hop(level, c, up):
        def go(low, count):
            ref = gathered.at[level, c, pl.ds(low, count)]
            send(ref, ref, g_send.at[level, int(up)], g_recv.at[level, c], me + w if up else me - w).start()

        held(z + 1 if up else z - 1, up, go)

    def hop_sent(level, up):
        held(z + 1 if up else z - 1, up, lambda low, count: pass_by(g_send.at[level, int(up)], gathered.at[level, :, pl.ds(low, count)]).wait())

    def hop_arrived(level, c, up):
        held(z, up, lambda low, count: pass_by(g_recv.at[level, c], gathered.at[level, c, pl.ds(low, count)]).wait())

    loads[0].wait()
    for r in range(responses):
        gathered[z, :, r] = prompts[of_ref[r]].reshape(chunks, part, DV)

    @pl.when(has_down)
    def _():
        for c in range(chunks):
            hop(z, c, False)

    last = z == planes - 1

    @pl.loop(0, 2 * w + 1)
    def _(i):
        c = 2 * z * w + i
        start = jnp.int32(0)
        begins = jnp.int32(0)
        which = jnp.int32(-1)
        for r in range(responses):
            begins = begins + jnp.where(start == c, 1, 0)
            which = which + jnp.where(start <= c, 1, 0)
            start = start + len_ref[r]
        flag[i] = begins
        index[i] = which

    started = jnp.where(last, index[0] + jnp.where(flag[0] > 0, 0, 1), 0)

    @pl.when(z == 0)
    def _():
        s_in[...] = jnp.zeros_like(s_in)

    second_starts = flag[2 * j + 1] > 0

    def columns(h):
        return pl.ds(pl.multiple_of(h * DK, DK), DK)

    low = jnp.where(last, 2, jnp.where(upper, 1, 0))

    def prompt(level, c, block, floor):
        which = index[block]
        chosen = jnp.zeros((part, DV), jnp.bfloat16)
        for i in range(some):
            r = jnp.minimum(low + i, responses - 1)
            chosen = jnp.where(jnp.logical_and(which == r, which >= floor), gathered[level, c, r], chosen)
        return chosen

    def make(level, c):
        for k in range(w):
            m = lax.rem(j + k, w)
            ref = d_in.at[level, j] if k == 0 else d_out.at[level, m]
            for block in range(2):
                ref[c, block] = prompt(level, c, 2 * m + block, started)

    def give(level, c):
        for k in range(1, w):
            m = lax.rem(j + k, w)
            send(d_out.at[level, m, c], d_in.at[level, j, c], d_send, d_recv.at[level, j], z * w + m).start()

    @pl.when(j < w - 1)
    def _():
        pl.semaphore_wait(ready_mate, w - 1 - j)

    loads[1].wait()
    loads[2].wait()

    def share(level, half, number):
        send(t_own.at[half, :, level], t_mate.at[half, :, level], t_send.at[number], t_recv.at[number, level], mate).start()

    @pl.loop(0, planes)
    def _(level):
        for i in range(per_level):
            h = level * per_level + i
            cols = columns(h)
            a = matmul(k_ref[0:SPAN, cols], v_ref[0:SPAN, cols], 0, 0)
            b = matmul(k_ref[SPAN:2 * SPAN, cols], v_ref[SPAN:2 * SPAN, cols], 0, 0)
            first[h] = a
            total = jnp.where(second_starts, b, a + b).astype(jnp.bfloat16)
            for p in range(pieces):
                column = i * pieces + p
                t_own[column % 2, column // 2, level] = total[p * rows:(p + 1) * rows]
        share(level, 1 - core, 0)

    @pl.when(has_up)
    def _():
        pl.semaphore_wait(ready_up, 1)
        for c in range(chunks):
            hop(z, c, True)

    late = flag[4 * x + 2] + flag[4 * x + 3] > 0

    @pl.loop(0, planes)
    def _(level):
        pass_by(t_recv.at[0, level], t_mate.at[core, :, level]).wait()
        for k in range(chips):
            to = lax.rem(x + k, chips)
            column = 2 * to + core
            own = t_own[core, to, level].astype(jnp.float32)
            other = t_mate[core, to, level].astype(jnp.float32)
            total = jnp.where(late, jnp.where(core == 1, own, other), own + other).astype(jnp.bfloat16)
            if k == 0:
                tc_in[x, level] = total
            else:
                tc_out[to, level] = total
                send(tc_out.at[to, level], tc_in.at[x, level], tc_send, tc_recv.at[x, level], z * w + column).start()

    for c in range(chunks):
        make(z, c)
        give(z, c)

    @pl.when(core == 0)
    def _():
        @pl.loop(0, planes)
        def _(level):
            share(level, 0, 1)

    loads[3].wait()
    causal = lax.broadcasted_iota(jnp.int32, (SPAN, SPAN), 0) >= lax.broadcasted_iota(jnp.int32, (SPAN, SPAN), 1)

    group = 4

    @pl.loop(0, heads, step=group)
    def _(base):
        parts = []
        for u in range(group):
            for block in range(2):
                parts.append((slice(block * SPAN, (block + 1) * SPAN), columns(base + u)))
        weights = [jnp.where(causal, matmul(q_ref[rng, cols], k_ref[rng, cols], 1, 1), 0.0).astype(jnp.bfloat16) for rng, cols in parts]
        for (rng, cols), weight in zip(parts, weights):
            intra[rng, cols] = matmul(weight, v_ref[rng, cols], 1, 0)

    def receive(level, c, up):
        hop_arrived(level, c, up)

        @pl.when(has_up if up else has_down)
        def _():
            hop(level, c, up)

    def both(distance, f):
        @pl.when(z + distance < planes)
        def _():
            f(z + distance, False)

        @pl.when(z - distance >= 0)
        def _():
            f(z - distance, True)

    def scan(level):
        for k in range(1, chips):
            other = lax.rem(x + k, chips)
            pass_by(tc_recv.at[other, level], tc_in.at[other, level]).wait()

        @pl.when(has_down)
        def _():
            pass_by(s_recv.at[level], s_in.at[level]).wait()

        state = s_in[level].astype(jnp.float32)
        for i in range(chips):
            state = jnp.where(flag[4 * i] > 0, 0.0, state)
            e_out[i, level] = state.astype(jnp.bfloat16)
            inside = flag[4 * i + 1] + flag[4 * i + 2] + flag[4 * i + 3]
            state = jnp.where(inside > 0, 0.0, state) + tc_in[i, level].astype(jnp.float32)

        @pl.when(z != planes - 2)
        def _():
            s_out[level] = state.astype(jnp.bfloat16)

        @pl.when(z == planes - 2)
        def _():
            for c in range(chunks):
                rng = slice(c * part, (c + 1) * part)
                s_out[level, rng] = (state[rng] + prompt(level, c, 2 * w, 0).astype(jnp.float32)).astype(jnp.bfloat16)

        @pl.when(has_up)
        def _():
            send(s_out.at[level], s_in.at[level], s_send, s_recv.at[level], me + w).start()

        for k in range(1, chips):
            to = lax.rem(x + k, chips)
            send(e_out.at[to, level], e_in.at[level, j], e_send.at[1], e_recv.at[level, j], z * w + 2 * to + core).start()
        e_in[level, j] = e_out[x, level]
        send(e_in.at[level, j], e_in.at[level, j], e_send.at[0], e_recv.at[level, j], mate).start()

    def relay(level):
        for k in range(1, chips):
            column = 2 * lax.rem(x + k, chips) + core
            pass_by(e_recv.at[level, column], e_in.at[level, column]).wait()
            send(e_in.at[level, column], e_in.at[level, column], e_send.at[2], e_recv.at[level, column], mate).start()

    def step(distance, c):
        both(distance, lambda level, up: receive(level, c, up))

        def pass_on(level, up):
            make(level, c)
            give(level, c)

        both(distance, pass_on)

    share_of = planes // chunks

    def some_levels(c, f):
        for i in range(share_of):
            f(c * share_of + i)

    def back(i):
        scan(planes - 1 - i)

    def steps(distance, before=None, after=None):
        @pl.loop(0, chunks)
        def _(c):
            if before is not None:
                pl.when(before(c))(lambda: some_levels(c, back))
            step(distance, c)
            if after is not None:
                pl.when(after(c))(lambda: some_levels(c, back))

    if planes == 4:
        steps(1, after=lambda c: z == 0)
        steps(2, before=lambda c: z == 1, after=lambda c: z == 2)
    else:
        steps(1, after=lambda c: z == 0)
        steps(2, after=lambda c: jnp.logical_and(z > 0, z < planes - 2))

        @pl.loop(3, planes - 2)
        def _(distance):
            steps(distance)

        steps(planes - 2, after=lambda c: z == planes - 2)

    @pl.when(z == 0)
    def _():
        pl.loop(0, planes)(lambda i: relay(planes - 1 - i))

    steps(planes - 1, before=lambda c: jnp.logical_and(last, c < chunks - 1), after=lambda c: jnp.logical_and(last, c == chunks - 1))

    fresh = jnp.logical_and(core == 1, flag[2 * j] == 0)
    open_end = jnp.logical_or(core == 0, flag[4 * x + 1] + flag[4 * x + 2] == 0)

    def finish(level, which):
        @pl.when(core == 1)
        def _():
            pass_by(t_recv.at[1, level], t_mate.at[0, :, level]).wait()

        for i in which:
            for o in range(i * pieces, (i + 1) * pieces):
                @pl.when(core != o % 2)
                def _():
                    pass_by(e_recv.at[level, o], e_in.at[level, o]).wait()

        for i in which:
            for o in range(pieces):
                owner = i * pieces + o

                @pl.when(owner != j)
                def _():
                    pass_by(d_recv.at[level, owner], d_in.at[level, owner]).wait()

        for i in which:
            cols = columns(level * per_level + i)
            entering = d_in[level, pl.ds(i * pieces, pieces), :, 0].reshape(DK, DV)
            second = d_in[level, pl.ds(i * pieces, pieces), :, 1].reshape(DK, DV)
            before = jnp.concatenate([t_mate[o % 2, o // 2, level] for o in range(i * pieces, (i + 1) * pieces)], axis=0)
            summed = e_in[level, pl.ds(i * pieces, pieces)].reshape(DK, DV).astype(jnp.float32)
            state = entering.astype(jnp.float32) + jnp.where(open_end, summed, 0.0) + jnp.where(fresh, before.astype(jnp.float32), 0.0)
            later = (state + first[level * per_level + i]).astype(jnp.bfloat16)
            at = (state.astype(jnp.bfloat16), jnp.where(second_starts, second, later))
            for block in range(2):
                rng = slice(block * SPAN, (block + 1) * SPAN)
                o = matmul(q_ref[rng, cols], at[block], 1, 0) + intra[rng, cols]
                scale = lax.rsqrt(jnp.mean(o * o, axis=-1, keepdims=True) + epsilon)
                out_ref[rng, cols] = (o * scale).astype(jnp.bfloat16)

    @pl.when(z == 0)
    def _():
        @pl.loop(0, planes)
        def _(level):
            finish(level, range(per_level))

    @pl.when(has_down)
    def _():
        ahead = 2

        @pl.loop(0, planes + ahead)
        def _(i):
            pl.when(i < planes)(lambda: relay(planes - 1 - i))
            pl.when(i >= ahead)(lambda: finish(planes - 1 + ahead - i, range(per_level)))

    pass_by(t_send.at[0], t_own.at[0]).wait()

    @pl.when(core == 0)
    def _():
        pass_by(t_send.at[1], t_own.at[0]).wait()

    pass_by(tc_send, tc_out.at[0:chips - 1]).wait()
    pass_by(e_send.at[0], s_out).wait()
    pass_by(e_send.at[1], e_out.at[0:chips - 1]).wait()
    pass_by(e_send.at[2], e_out.at[0:chips - 1]).wait()
    pass_by(d_send, d_out.at[:, 0:w - 1]).wait()

    @pl.when(has_up)
    def _():
        pass_by(s_send, s_out).wait()

        @pl.loop(0, z + 1)
        def _(level):
            hop_sent(level, True)

    @pl.when(has_down)
    def _():
        @pl.loop(z, planes)
        def _(level):
            hop_sent(level, False)


def solution(mesh):
    n = mesh.shape["seq"]

    def shards(queries, keys, values, prompt_state, lengths, prompt_of):
        tokens, width = queries.shape
        count, rows, _ = prompt_state.shape
        half = jnp.bfloat16
        w = plane_width(n)
        planes = n // w
        chunks = max(1, rows // 32)
        part = rows // chunks
        anywhere = pl.BlockSpec(memory_space=pl.ANY)
        scalar = pl.BlockSpec(memory_space=pltpu.SMEM)
        dma = pltpu.SemaphoreType.DMA
        regular = pltpu.SemaphoreType.REGULAR
        spread = pltpu.VMEM((planes, w, chunks, 2, part, DV), half)
        sums = pltpu.VMEM((2, w // 2, planes, rows, DV), half)
        chips = pltpu.VMEM((w // 2, planes, rows, DV), half)
        chain = pltpu.VMEM((planes, rows, DV), half)
        block = pltpu.VMEM((tokens, width), half)
        return pl.pallas_call(
            functools.partial(kernel, n),
            out_shape=pltpu.VMEM((tokens, width), half),
            in_specs=[anywhere] * 4 + [scalar] * 2,
            out_specs=pl.BlockSpec(memory_space=pltpu.VMEM),
            scratch_shapes=[
                block, block, block,
                pltpu.VMEM((count, rows, DV), half),
                pltpu.VMEM((tokens, width), jnp.float32),
                pltpu.VMEM((width // DK, DK, DV), jnp.float32),
                pltpu.VMEM((planes, chunks, lengths.shape[0], part, DV), half),
                sums, sums, chips, chips, chain, chain,
                chips, pltpu.VMEM((planes, w, rows, DV), half),
                spread, spread,
                pltpu.SMEM((2 * w + 1,), jnp.int32),
                pltpu.SMEM((2 * w + 1,), jnp.int32),
                regular, regular,
                dma((4,)), dma((planes, 2)), dma((planes, chunks)), dma((2,)), dma((2, planes)),
                dma(()), dma((w // 2, planes)),
                dma(()), dma((planes,)), dma((3,)), dma((planes, w)), dma(()), dma((planes, w)),
            ],
            compiler_params=pltpu.CompilerParams(
                collective_id=0, has_side_effects=True, vmem_limit_bytes=62 << 20),
        )(queries, keys, values, prompt_state, lengths, prompt_of.reshape(-1))

    placed = (
        P(("groups", "seq"), None),
        P(("groups", "seq"), None),
        P(("groups", "seq"), None),
        P("groups", "seq", None),
        P("groups"),
        P("groups", None),
    )
    return jax.shard_map(
        shards, mesh=mesh, in_specs=placed, out_specs=P(("groups", "seq"), None), check_vma=False
    )
```

```python
import functools
import jax
import jax.numpy as jnp
from jax import lax
from jax.experimental import pallas as pl
from jax.experimental.pallas import tpu as pltpu
from jax.sharding import PartitionSpec as P

DK = 128
DV = 128
SPAN = 128
epsilon = 1e-06


def matmul(a, b, ca, cb):
    return lax.dot_general(a, b, (((ca,), (cb,)), ((), ())), preferred_element_type=jnp.float32)


def plane_width(n):
    x = 1
    while (2 * x) ** 3 <= n // 2:
        x *= 2
    return 2 * x


def kernel(n, q_hbm, k_hbm, v_hbm, p_hbm, len_ref, of_ref, out_ref,
           q_ref, k_ref, v_ref, prompts, intra, first, gathered, t_own, t_mate, tc_out, tc_in, s_out, s_in, e_out, e_in, d_out, d_in, flag, index,
           ready_up, ready_mate, load_sem, g_send, g_recv, t_send, t_recv, tc_send, tc_recv, s_send, s_recv, e_send, e_recv, d_send, d_recv):
    me = lax.axis_index("seq")
    w = plane_width(n)
    planes = n // w
    z = me // w
    j = lax.rem(me, w)
    upper = 2 * z >= planes
    chips = w // 2
    x = j // 2
    core = lax.rem(j, 2)
    mate = me + 1 - 2 * core
    heads = k_ref.shape[1] // DK
    rows = prompts.shape[1]
    pieces = DK // rows
    per_level = w // pieces
    _, chunks, responses, part, _ = gathered.shape
    some = responses - 1

    def load(i, src, dst):
        return pltpu.make_async_copy(src, dst, load_sem.at[i])

    loads = [load(0, p_hbm, prompts), load(1, k_hbm, k_ref), load(2, v_hbm, v_ref), load(3, q_hbm, q_ref)]
    for copy in loads:
        copy.start()

    def signal(sem, device):
        pl.semaphore_signal(sem, inc=1, device_id={"seq": device}, device_id_type=pl.DeviceIdType.MESH)

    def send(src, dst, send_sem, recv_sem, target):
        return pltpu.make_async_remote_copy(
            src_ref=src, dst_ref=dst, send_sem=send_sem, recv_sem=recv_sem,
            device_id={"seq": target}, device_id_type=pl.DeviceIdType.MESH)

    def pass_by(sem, ref):
        return pltpu.make_async_copy(ref, ref, sem)

    barrier = pltpu.get_barrier_semaphore()
    has_up = z < planes - 1
    has_down = z > 0

    @pl.when(has_up)
    def _():
        signal(barrier, me + w)

    @pl.loop(j + 1, w)
    def _(m):
        signal(barrier, z * w + m)

    @pl.when(me > 0)
    def _():
        pl.semaphore_wait(barrier, j + jnp.where(has_down, 1, 0))

    @pl.when(has_down)
    def _():
        signal(ready_up, me - w)

    @pl.loop(0, j)
    def _(m):
        signal(ready_mate, z * w + m)

    def held(plane, up, f):
        if up:
            last = plane == planes - 1
            pl.when(2 * plane < planes)(lambda: f(0, responses))
            pl.when(jnp.logical_and(2 * plane >= planes, jnp.logical_not(last)))(lambda: f(1, responses - 1))
            pl.when(last)(lambda: f(2, responses - 2))
        else:
            pl.when(2 * plane < planes)(lambda: f(0, responses - 1))
            pl.when(2 * plane >= planes)(lambda: f(0, responses))

    def hop(level, c, up):
        def go(low, count):
            ref = gathered.at[level, c, pl.ds(low, count)]
            send(ref, ref, g_send.at[level, int(up)], g_recv.at[level, c], me + w if up else me - w).start()

        held(z + 1 if up else z - 1, up, go)

    def hop_sent(level, up):
        held(z + 1 if up else z - 1, up, lambda low, count: pass_by(g_send.at[level, int(up)], gathered.at[level, :, pl.ds(low, count)]).wait())

    def hop_arrived(level, c, up):
        held(z, up, lambda low, count: pass_by(g_recv.at[level, c], gathered.at[level, c, pl.ds(low, count)]).wait())

    loads[0].wait()
    for r in range(responses):
        gathered[z, :, r] = prompts[of_ref[r]].reshape(chunks, part, DV)

    @pl.when(has_down)
    def _():
        for c in range(chunks):
            hop(z, c, False)

    last = z == planes - 1

    @pl.loop(0, 2 * w + 1)
    def _(i):
        c = 2 * z * w + i
        start = jnp.int32(0)
        begins = jnp.int32(0)
        which = jnp.int32(-1)
        for r in range(responses):
            begins = begins + jnp.where(start == c, 1, 0)
            which = which + jnp.where(start <= c, 1, 0)
            start = start + len_ref[r]
        flag[i] = begins
        index[i] = which

    started = jnp.where(last, index[0] + jnp.where(flag[0] > 0, 0, 1), 0)

    @pl.when(z == 0)
    def _():
        s_in[...] = jnp.zeros_like(s_in)

    second_starts = flag[2 * j + 1] > 0

    def columns(h):
        return pl.ds(pl.multiple_of(h * DK, DK), DK)

    low = jnp.where(last, 2, jnp.where(upper, 1, 0))

    def prompt(level, c, block, floor):
        which = index[block]
        chosen = jnp.zeros((part, DV), jnp.bfloat16)
        for i in range(some):
            r = jnp.minimum(low + i, responses - 1)
            chosen = jnp.where(jnp.logical_and(which == r, which >= floor), gathered[level, c, r], chosen)
        return chosen

    def make(level, c):
        for k in range(w):
            m = lax.rem(j + k, w)
            ref = d_in.at[level, j] if k == 0 else d_out.at[level, m]
            for block in range(2):
                ref[c, block] = prompt(level, c, 2 * m + block, started)

    def give(level, c):
        for k in range(1, w):
            m = lax.rem(j + k, w)
            send(d_out.at[level, m, c], d_in.at[level, j, c], d_send, d_recv.at[level, j], z * w + m).start()

    @pl.when(j < w - 1)
    def _():
        pl.semaphore_wait(ready_mate, w - 1 - j)

    @pl.when(has_up)
    def _():
        pl.semaphore_wait(ready_up, 1)
        for c in range(chunks):
            hop(z, c, True)

    loads[1].wait()
    loads[2].wait()

    def share(level, half, number):
        send(t_own.at[half, :, level], t_mate.at[half, :, level], t_send.at[number], t_recv.at[number, level], mate).start()

    @pl.loop(0, planes)
    def _(level):
        for i in range(per_level):
            h = level * per_level + i
            cols = columns(h)
            a = matmul(k_ref[0:SPAN, cols], v_ref[0:SPAN, cols], 0, 0)
            b = matmul(k_ref[SPAN:2 * SPAN, cols], v_ref[SPAN:2 * SPAN, cols], 0, 0)
            first[h] = a
            total = jnp.where(second_starts, b, a + b).astype(jnp.bfloat16)
            for p in range(pieces):
                column = i * pieces + p
                t_own[column % 2, column // 2, level] = total[p * rows:(p + 1) * rows]
        share(level, 1 - core, 0)

    late = flag[4 * x + 2] + flag[4 * x + 3] > 0

    @pl.loop(0, planes)
    def _(level):
        pass_by(t_recv.at[0, level], t_mate.at[core, :, level]).wait()
        for k in range(chips):
            to = lax.rem(x + k, chips)
            column = 2 * to + core
            own = t_own[core, to, level].astype(jnp.float32)
            other = t_mate[core, to, level].astype(jnp.float32)
            total = jnp.where(late, jnp.where(core == 1, own, other), own + other).astype(jnp.bfloat16)
            if k == 0:
                tc_in[x, level] = total
            else:
                tc_out[to, level] = total
                send(tc_out.at[to, level], tc_in.at[x, level], tc_send, tc_recv.at[x, level], z * w + column).start()

    for c in range(chunks):
        make(z, c)
        give(z, c)

    @pl.when(core == 0)
    def _():
        @pl.loop(0, planes)
        def _(level):
            share(level, 0, 1)

    loads[3].wait()
    causal = lax.broadcasted_iota(jnp.int32, (SPAN, SPAN), 0) >= lax.broadcasted_iota(jnp.int32, (SPAN, SPAN), 1)

    group = 4

    @pl.loop(0, heads, step=group)
    def _(base):
        parts = []
        for u in range(group):
            for block in range(2):
                parts.append((slice(block * SPAN, (block + 1) * SPAN), columns(base + u)))
        weights = [jnp.where(causal, matmul(q_ref[rng, cols], k_ref[rng, cols], 1, 1), 0.0).astype(jnp.bfloat16) for rng, cols in parts]
        for (rng, cols), weight in zip(parts, weights):
            intra[rng, cols] = matmul(weight, v_ref[rng, cols], 1, 0)

    def receive(level, c, up):
        hop_arrived(level, c, up)

        @pl.when(has_up if up else has_down)
        def _():
            hop(level, c, up)

    def both(distance, f):
        @pl.when(z + distance < planes)
        def _():
            f(z + distance, False)

        @pl.when(z - distance >= 0)
        def _():
            f(z - distance, True)

    def scan(level):
        for k in range(1, chips):
            other = lax.rem(x + k, chips)
            pass_by(tc_recv.at[other, level], tc_in.at[other, level]).wait()

        @pl.when(has_down)
        def _():
            pass_by(s_recv.at[level], s_in.at[level]).wait()

        state = s_in[level].astype(jnp.float32)
        for i in range(chips):
            state = jnp.where(flag[4 * i] > 0, 0.0, state)
            e_out[i, level] = state.astype(jnp.bfloat16)
            inside = flag[4 * i + 1] + flag[4 * i + 2] + flag[4 * i + 3]
            state = jnp.where(inside > 0, 0.0, state) + tc_in[i, level].astype(jnp.float32)

        @pl.when(z != planes - 2)
        def _():
            s_out[level] = state.astype(jnp.bfloat16)

        @pl.when(z == planes - 2)
        def _():
            for c in range(chunks):
                rng = slice(c * part, (c + 1) * part)
                s_out[level, rng] = (state[rng] + prompt(level, c, 2 * w, 0).astype(jnp.float32)).astype(jnp.bfloat16)

        @pl.when(has_up)
        def _():
            send(s_out.at[level], s_in.at[level], s_send, s_recv.at[level], me + w).start()

        for k in range(1, chips):
            to = lax.rem(x + k, chips)
            send(e_out.at[to, level], e_in.at[level, j], e_send.at[1], e_recv.at[level, j], z * w + 2 * to + core).start()
        e_in[level, j] = e_out[x, level]
        send(e_in.at[level, j], e_in.at[level, j], e_send.at[0], e_recv.at[level, j], mate).start()

    def relay(level):
        for k in range(1, chips):
            column = 2 * lax.rem(x + k, chips) + core
            pass_by(e_recv.at[level, column], e_in.at[level, column]).wait()
            send(e_in.at[level, column], e_in.at[level, column], e_send.at[2], e_recv.at[level, column], mate).start()

    def step(distance, c):
        both(distance, lambda level, up: receive(level, c, up))

        def pass_on(level, up):
            make(level, c)
            give(level, c)

        both(distance, pass_on)

    share_of = planes // chunks

    def some_levels(c, f):
        for i in range(share_of):
            f(c * share_of + i)

    def back(i):
        scan(planes - 1 - i)

    def steps(distance, before=None, after=None):
        @pl.loop(0, chunks)
        def _(c):
            if before is not None:
                pl.when(before(c))(lambda: some_levels(c, back))
            step(distance, c)
            if after is not None:
                pl.when(after(c))(lambda: some_levels(c, back))

    if planes == 4:
        steps(1, after=lambda c: z == 0)
        steps(2, before=lambda c: z == 1, after=lambda c: z == 2)
    else:
        steps(1, after=lambda c: z == 0)
        steps(2, after=lambda c: jnp.logical_and(z > 0, z < planes - 2))

        @pl.loop(3, planes - 2)
        def _(distance):
            steps(distance)

        steps(planes - 2, after=lambda c: z == planes - 2)

    @pl.when(z == 0)
    def _():
        pl.loop(0, planes)(lambda i: relay(planes - 1 - i))

    steps(planes - 1, before=lambda c: last)

    fresh = jnp.logical_and(core == 1, flag[2 * j] == 0)
    open_end = jnp.logical_or(core == 0, flag[4 * x + 1] + flag[4 * x + 2] == 0)

    def finish(level, which):
        @pl.when(core == 1)
        def _():
            pass_by(t_recv.at[1, level], t_mate.at[0, :, level]).wait()

        for i in which:
            for o in range(i * pieces, (i + 1) * pieces):
                @pl.when(core != o % 2)
                def _():
                    pass_by(e_recv.at[level, o], e_in.at[level, o]).wait()

        for i in which:
            for o in range(pieces):
                owner = i * pieces + o

                @pl.when(owner != j)
                def _():
                    pass_by(d_recv.at[level, owner], d_in.at[level, owner]).wait()

        for i in which:
            cols = columns(level * per_level + i)
            entering = d_in[level, pl.ds(i * pieces, pieces), :, 0].reshape(DK, DV)
            second = d_in[level, pl.ds(i * pieces, pieces), :, 1].reshape(DK, DV)
            before = jnp.concatenate([t_mate[o % 2, o // 2, level] for o in range(i * pieces, (i + 1) * pieces)], axis=0)
            summed = e_in[level, pl.ds(i * pieces, pieces)].reshape(DK, DV).astype(jnp.float32)
            state = entering.astype(jnp.float32) + jnp.where(open_end, summed, 0.0) + jnp.where(fresh, before.astype(jnp.float32), 0.0)
            later = (state + first[level * per_level + i]).astype(jnp.bfloat16)
            at = (state.astype(jnp.bfloat16), jnp.where(second_starts, second, later))
            for block in range(2):
                rng = slice(block * SPAN, (block + 1) * SPAN)
                o = matmul(q_ref[rng, cols], at[block], 1, 0) + intra[rng, cols]
                scale = lax.rsqrt(jnp.mean(o * o, axis=-1, keepdims=True) + epsilon)
                out_ref[rng, cols] = (o * scale).astype(jnp.bfloat16)

    @pl.when(z == 0)
    def _():
        @pl.loop(0, planes)
        def _(level):
            finish(level, range(per_level))

    @pl.when(has_down)
    def _():
        ahead = 2

        @pl.loop(0, planes + ahead)
        def _(i):
            pl.when(i < planes)(lambda: relay(planes - 1 - i))
            pl.when(i >= ahead)(lambda: finish(planes - 1 + ahead - i, range(per_level)))

    pass_by(t_send.at[0], t_own.at[0]).wait()

    @pl.when(core == 0)
    def _():
        pass_by(t_send.at[1], t_own.at[0]).wait()

    pass_by(tc_send, tc_out.at[0:chips - 1]).wait()
    pass_by(e_send.at[0], s_out).wait()
    pass_by(e_send.at[1], e_out.at[0:chips - 1]).wait()
    pass_by(e_send.at[2], e_out.at[0:chips - 1]).wait()
    pass_by(d_send, d_out.at[:, 0:w - 1]).wait()

    @pl.when(has_up)
    def _():
        pass_by(s_send, s_out).wait()

        @pl.loop(0, z + 1)
        def _(level):
            hop_sent(level, True)

    @pl.when(has_down)
    def _():
        @pl.loop(z, planes)
        def _(level):
            hop_sent(level, False)


def solution(mesh):
    n = mesh.shape["seq"]

    def shards(queries, keys, values, prompt_state, lengths, prompt_of):
        tokens, width = queries.shape
        count, rows, _ = prompt_state.shape
        half = jnp.bfloat16
        w = plane_width(n)
        planes = n // w
        chunks = max(1, rows // 64)
        part = rows // chunks
        anywhere = pl.BlockSpec(memory_space=pl.ANY)
        scalar = pl.BlockSpec(memory_space=pltpu.SMEM)
        dma = pltpu.SemaphoreType.DMA
        regular = pltpu.SemaphoreType.REGULAR
        spread = pltpu.VMEM((planes, w, chunks, 2, part, DV), half)
        sums = pltpu.VMEM((2, w // 2, planes, rows, DV), half)
        chips = pltpu.VMEM((w // 2, planes, rows, DV), half)
        chain = pltpu.VMEM((planes, rows, DV), half)
        block = pltpu.VMEM((tokens, width), half)
        return pl.pallas_call(
            functools.partial(kernel, n),
            out_shape=pltpu.VMEM((tokens, width), half),
            in_specs=[anywhere] * 4 + [scalar] * 2,
            out_specs=pl.BlockSpec(memory_space=pltpu.VMEM),
            scratch_shapes=[
                block, block, block,
                pltpu.VMEM((count, rows, DV), half),
                pltpu.VMEM((tokens, width), jnp.float32),
                pltpu.VMEM((width // DK, DK, DV), jnp.float32),
                pltpu.VMEM((planes, chunks, lengths.shape[0], part, DV), half),
                sums, sums, chips, chips, chain, chain,
                chips, pltpu.VMEM((planes, w, rows, DV), half),
                spread, spread,
                pltpu.SMEM((2 * w + 1,), jnp.int32),
                pltpu.SMEM((2 * w + 1,), jnp.int32),
                regular, regular,
                dma((4,)), dma((planes, 2)), dma((planes, chunks)), dma((2,)), dma((2, planes)),
                dma(()), dma((w // 2, planes)),
                dma(()), dma((planes,)), dma((3,)), dma((planes, w)), dma(()), dma((planes, w)),
            ],
            compiler_params=pltpu.CompilerParams(
                collective_id=0, has_side_effects=True, vmem_limit_bytes=62 << 20),
        )(queries, keys, values, prompt_state, lengths, prompt_of.reshape(-1))

    placed = (
        P(("groups", "seq"), None),
        P(("groups", "seq"), None),
        P(("groups", "seq"), None),
        P("groups", "seq", None),
        P("groups"),
        P("groups", None),
    )
    return jax.shard_map(
        shards, mesh=mesh, in_specs=placed, out_specs=P(("groups", "seq"), None), check_vma=False
    )
```

```python
import functools
import jax
import jax.numpy as jnp
from jax import lax
from jax.experimental import pallas as pl
from jax.experimental.pallas import tpu as pltpu
from jax.sharding import PartitionSpec as P

DK = 128
DV = 128
SPAN = 128
epsilon = 1e-06


def matmul(a, b, ca, cb):
    return lax.dot_general(a, b, (((ca,), (cb,)), ((), ())), preferred_element_type=jnp.float32)


def plane_width(n):
    x = 1
    while (2 * x) ** 3 <= n // 2:
        x *= 2
    return 2 * x


def kernel(n, q_hbm, k_hbm, v_hbm, p_hbm, len_ref, of_ref, out_ref,
           q_ref, k_ref, v_ref, prompts, intra, first, gathered, t_own, t_mate, tc_out, tc_in, s_out, s_in, e_out, e_in, d_out, d_in, flag, index,
           ready_up, ready_mate, load_sem, g_send, g_recv, t_send, t_recv, tc_send, tc_recv, s_send, s_recv, e_send, e_recv, d_send, d_recv):
    me = lax.axis_index("seq")
    w = plane_width(n)
    planes = n // w
    z = me // w
    j = lax.rem(me, w)
    upper = 2 * z >= planes
    chips = w // 2
    x = j // 2
    core = lax.rem(j, 2)
    mate = me + 1 - 2 * core
    heads = k_ref.shape[1] // DK
    rows = prompts.shape[1]
    pieces = DK // rows
    per_level = w // pieces
    _, chunks, responses, part, _ = gathered.shape
    some = responses - 1

    def load(i, src, dst):
        return pltpu.make_async_copy(src, dst, load_sem.at[i])

    loads = [load(0, p_hbm, prompts), load(1, k_hbm, k_ref), load(2, v_hbm, v_ref), load(3, q_hbm, q_ref)]
    for copy in loads:
        copy.start()

    def signal(sem, device):
        pl.semaphore_signal(sem, inc=1, device_id={"seq": device}, device_id_type=pl.DeviceIdType.MESH)

    def send(src, dst, send_sem, recv_sem, target):
        return pltpu.make_async_remote_copy(
            src_ref=src, dst_ref=dst, send_sem=send_sem, recv_sem=recv_sem,
            device_id={"seq": target}, device_id_type=pl.DeviceIdType.MESH)

    def pass_by(sem, ref):
        return pltpu.make_async_copy(ref, ref, sem)

    barrier = pltpu.get_barrier_semaphore()
    has_up = z < planes - 1
    has_down = z > 0

    @pl.when(has_up)
    def _():
        signal(barrier, me + w)

    @pl.loop(j + 1, w)
    def _(m):
        signal(barrier, z * w + m)

    @pl.when(me > 0)
    def _():
        pl.semaphore_wait(barrier, j + jnp.where(has_down, 1, 0))

    @pl.when(has_down)
    def _():
        signal(ready_up, me - w)

    @pl.loop(0, j)
    def _(m):
        signal(ready_mate, z * w + m)

    def held(plane, up, f):
        if up:
            last = plane == planes - 1
            pl.when(2 * plane < planes)(lambda: f(0, responses))
            pl.when(jnp.logical_and(2 * plane >= planes, jnp.logical_not(last)))(lambda: f(1, responses - 1))
            pl.when(last)(lambda: f(2, responses - 2))
        else:
            pl.when(2 * plane < planes)(lambda: f(0, responses - 1))
            pl.when(2 * plane >= planes)(lambda: f(0, responses))

    def hop(level, c, up):
        def go(low, count):
            ref = gathered.at[level, c, pl.ds(low, count)]
            send(ref, ref, g_send.at[level, int(up)], g_recv.at[level, c], me + w if up else me - w).start()

        held(z + 1 if up else z - 1, up, go)

    def hop_sent(level, up):
        held(z + 1 if up else z - 1, up, lambda low, count: pass_by(g_send.at[level, int(up)], gathered.at[level, :, pl.ds(low, count)]).wait())

    def hop_arrived(level, c, up):
        held(z, up, lambda low, count: pass_by(g_recv.at[level, c], gathered.at[level, c, pl.ds(low, count)]).wait())

    loads[0].wait()
    for r in range(responses):
        gathered[z, :, r] = prompts[of_ref[r]].reshape(chunks, part, DV)

    @pl.when(has_down)
    def _():
        for c in range(chunks):
            hop(z, c, False)

    last = z == planes - 1

    @pl.loop(0, 2 * w + 1)
    def _(i):
        c = 2 * z * w + i
        start = jnp.int32(0)
        begins = jnp.int32(0)
        which = jnp.int32(-1)
        for r in range(responses):
            begins = begins + jnp.where(start == c, 1, 0)
            which = which + jnp.where(start <= c, 1, 0)
            start = start + len_ref[r]
        flag[i] = begins
        index[i] = which

    started = jnp.where(last, index[0] + jnp.where(flag[0] > 0, 0, 1), 0)

    @pl.when(z == 0)
    def _():
        s_in[...] = jnp.zeros_like(s_in)

    second_starts = flag[2 * j + 1] > 0

    def columns(h):
        return pl.ds(pl.multiple_of(h * DK, DK), DK)

    low = jnp.where(last, 2, jnp.where(upper, 1, 0))

    def prompt(level, c, block, floor):
        which = index[block]
        chosen = jnp.zeros((part, DV), jnp.bfloat16)
        for i in range(some):
            r = jnp.minimum(low + i, responses - 1)
            chosen = jnp.where(jnp.logical_and(which == r, which >= floor), gathered[level, c, r], chosen)
        return chosen

    def make(level, c):
        for k in range(w):
            m = lax.rem(j + k, w)
            ref = d_in.at[level, j] if k == 0 else d_out.at[level, m]
            for block in range(2):
                ref[c, block] = prompt(level, c, 2 * m + block, started)

    def give(level, c):
        for k in range(1, w):
            m = lax.rem(j + k, w)
            send(d_out.at[level, m, c], d_in.at[level, j, c], d_send, d_recv.at[level, j], z * w + m).start()

    @pl.when(j < w - 1)
    def _():
        pl.semaphore_wait(ready_mate, w - 1 - j)

    @pl.when(has_up)
    def _():
        pl.semaphore_wait(ready_up, 1)
        for c in range(chunks):
            hop(z, c, True)

    loads[1].wait()
    loads[2].wait()

    def share(level, half, number):
        send(t_own.at[half, :, level], t_mate.at[half, :, level], t_send.at[number], t_recv.at[number, level], mate).start()

    @pl.loop(0, planes)
    def _(level):
        for i in range(per_level):
            h = level * per_level + i
            cols = columns(h)
            a = matmul(k_ref[0:SPAN, cols], v_ref[0:SPAN, cols], 0, 0)
            b = matmul(k_ref[SPAN:2 * SPAN, cols], v_ref[SPAN:2 * SPAN, cols], 0, 0)
            first[h] = a
            total = jnp.where(second_starts, b, a + b).astype(jnp.bfloat16)
            for p in range(pieces):
                column = i * pieces + p
                t_own[column % 2, column // 2, level] = total[p * rows:(p + 1) * rows]
        share(level, 1 - core, 0)

    late = flag[4 * x + 2] + flag[4 * x + 3] > 0
    needed = jnp.logical_or(has_up, x < chips - 1)

    @pl.loop(0, planes)
    def _(level):
        pass_by(t_recv.at[0, level], t_mate.at[core, :, level]).wait()
        for k in range(chips):
            to = lax.rem(x + k, chips)
            column = 2 * to + core
            own = t_own[core, to, level].astype(jnp.float32)
            other = t_mate[core, to, level].astype(jnp.float32)
            total = jnp.where(late, jnp.where(core == 1, own, other), own + other).astype(jnp.bfloat16)
            if k == 0:
                tc_in[x, level] = total
            else:
                tc_out[to, level] = total

                @pl.when(needed)
                def _():
                    send(tc_out.at[to, level], tc_in.at[x, level], tc_send, tc_recv.at[x, level], z * w + column).start()

    for c in range(chunks):
        make(z, c)
        give(z, c)

    @pl.when(core == 0)
    def _():
        @pl.loop(0, planes)
        def _(level):
            share(level, 0, 1)

    loads[3].wait()
    causal = lax.broadcasted_iota(jnp.int32, (SPAN, SPAN), 0) >= lax.broadcasted_iota(jnp.int32, (SPAN, SPAN), 1)

    group = 4

    @pl.loop(0, heads, step=group)
    def _(base):
        parts = []
        for u in range(group):
            for block in range(2):
                parts.append((slice(block * SPAN, (block + 1) * SPAN), columns(base + u)))
        weights = [jnp.where(causal, matmul(q_ref[rng, cols], k_ref[rng, cols], 1, 1), 0.0).astype(jnp.bfloat16) for rng, cols in parts]
        for (rng, cols), weight in zip(parts, weights):
            intra[rng, cols] = matmul(weight, v_ref[rng, cols], 1, 0)

    def receive(level, c, up):
        hop_arrived(level, c, up)

        @pl.when(has_up if up else has_down)
        def _():
            hop(level, c, up)

    def both(distance, f):
        @pl.when(z + distance < planes)
        def _():
            f(z + distance, False)

        @pl.when(z - distance >= 0)
        def _():
            f(z - distance, True)

    def scan(level):
        for k in range(1, chips):
            other = lax.rem(x + k, chips)

            @pl.when(jnp.logical_or(has_up, other < chips - 1))
            def _():
                pass_by(tc_recv.at[other, level], tc_in.at[other, level]).wait()

        @pl.when(has_down)
        def _():
            pass_by(s_recv.at[level], s_in.at[level]).wait()

        state = s_in[level].astype(jnp.float32)
        for i in range(chips):
            state = jnp.where(flag[4 * i] > 0, 0.0, state)
            e_out[i, level] = state.astype(jnp.bfloat16)
            inside = flag[4 * i + 1] + flag[4 * i + 2] + flag[4 * i + 3]
            state = jnp.where(inside > 0, 0.0, state) + tc_in[i, level].astype(jnp.float32)

        @pl.when(z != planes - 2)
        def _():
            s_out[level] = state.astype(jnp.bfloat16)

        @pl.when(z == planes - 2)
        def _():
            for c in range(chunks):
                rng = slice(c * part, (c + 1) * part)
                s_out[level, rng] = (state[rng] + prompt(level, c, 2 * w, 0).astype(jnp.float32)).astype(jnp.bfloat16)

        @pl.when(has_up)
        def _():
            send(s_out.at[level], s_in.at[level], s_send, s_recv.at[level], me + w).start()

        for k in range(1, chips):
            to = lax.rem(x + k, chips)
            send(e_out.at[to, level], e_in.at[level, j], e_send.at[1], e_recv.at[level, j], z * w + 2 * to + core).start()
        e_in[level, j] = e_out[x, level]
        send(e_in.at[level, j], e_in.at[level, j], e_send.at[0], e_recv.at[level, j], mate).start()

    def relay(level):
        for k in range(1, chips):
            column = 2 * lax.rem(x + k, chips) + core
            pass_by(e_recv.at[level, column], e_in.at[level, column]).wait()
            send(e_in.at[level, column], e_in.at[level, column], e_send.at[2], e_recv.at[level, column], mate).start()

    def step(distance, c):
        both(distance, lambda level, up: receive(level, c, up))

        def pass_on(level, up):
            make(level, c)
            give(level, c)

        both(distance, pass_on)

    share_of = planes // chunks

    def some_levels(c, f):
        for i in range(share_of):
            f(c * share_of + i)

    def back(i):
        scan(planes - 1 - i)

    def steps(distance, before=None, after=None):
        @pl.loop(0, chunks)
        def _(c):
            if before is not None:
                pl.when(before(c))(lambda: some_levels(c, back))
            step(distance, c)
            if after is not None:
                pl.when(after(c))(lambda: some_levels(c, back))

    if planes == 4:
        steps(1, after=lambda c: z == 0)
        steps(2, before=lambda c: z == 1, after=lambda c: z == 2)
    else:
        steps(1, after=lambda c: z == 0)
        steps(2, after=lambda c: jnp.logical_and(z > 0, z < planes - 2))

        @pl.loop(3, planes - 2)
        def _(distance):
            steps(distance)

        steps(planes - 2, after=lambda c: z == planes - 2)

    @pl.when(z == 0)
    def _():
        pl.loop(0, planes)(lambda i: relay(planes - 1 - i))

    steps(planes - 1, before=lambda c: last)

    fresh = jnp.logical_and(core == 1, flag[2 * j] == 0)
    open_end = jnp.logical_or(core == 0, flag[4 * x + 1] + flag[4 * x + 2] == 0)

    def finish(level, which):
        @pl.when(core == 1)
        def _():
            pass_by(t_recv.at[1, level], t_mate.at[0, :, level]).wait()

        for i in which:
            for o in range(i * pieces, (i + 1) * pieces):
                @pl.when(core != o % 2)
                def _():
                    pass_by(e_recv.at[level, o], e_in.at[level, o]).wait()

        for i in which:
            for o in range(pieces):
                owner = i * pieces + o

                @pl.when(owner != j)
                def _():
                    pass_by(d_recv.at[level, owner], d_in.at[level, owner]).wait()

        for i in which:
            cols = columns(level * per_level + i)
            entering = d_in[level, pl.ds(i * pieces, pieces), :, 0].reshape(DK, DV)
            second = d_in[level, pl.ds(i * pieces, pieces), :, 1].reshape(DK, DV)
            before = jnp.concatenate([t_mate[o % 2, o // 2, level] for o in range(i * pieces, (i + 1) * pieces)], axis=0)
            summed = e_in[level, pl.ds(i * pieces, pieces)].reshape(DK, DV).astype(jnp.float32)
            state = entering.astype(jnp.float32) + jnp.where(open_end, summed, 0.0) + jnp.where(fresh, before.astype(jnp.float32), 0.0)
            later = (state + first[level * per_level + i]).astype(jnp.bfloat16)
            at = (state.astype(jnp.bfloat16), jnp.where(second_starts, second, later))
            for block in range(2):
                rng = slice(block * SPAN, (block + 1) * SPAN)
                o = matmul(q_ref[rng, cols], at[block], 1, 0) + intra[rng, cols]
                scale = lax.rsqrt(jnp.mean(o * o, axis=-1, keepdims=True) + epsilon)
                out_ref[rng, cols] = (o * scale).astype(jnp.bfloat16)

    @pl.when(z == 0)
    def _():
        @pl.loop(0, planes)
        def _(level):
            finish(level, range(per_level))

    @pl.when(has_down)
    def _():
        ahead = 2

        @pl.loop(0, planes + ahead)
        def _(i):
            pl.when(i < planes)(lambda: relay(planes - 1 - i))
            pl.when(i >= ahead)(lambda: finish(planes - 1 + ahead - i, range(per_level)))

    pass_by(t_send.at[0], t_own.at[0]).wait()

    @pl.when(core == 0)
    def _():
        pass_by(t_send.at[1], t_own.at[0]).wait()


    @pl.when(needed)
    def _():
        pass_by(tc_send, tc_out.at[0:chips - 1]).wait()

    pass_by(e_send.at[0], s_out).wait()
    pass_by(e_send.at[1], e_out.at[0:chips - 1]).wait()
    pass_by(e_send.at[2], e_out.at[0:chips - 1]).wait()
    pass_by(d_send, d_out.at[:, 0:w - 1]).wait()

    @pl.when(has_up)
    def _():
        pass_by(s_send, s_out).wait()

        @pl.loop(0, z + 1)
        def _(level):
            hop_sent(level, True)

    @pl.when(has_down)
    def _():
        @pl.loop(z, planes)
        def _(level):
            hop_sent(level, False)


def solution(mesh):
    n = mesh.shape["seq"]

    def shards(queries, keys, values, prompt_state, lengths, prompt_of):
        tokens, width = queries.shape
        count, rows, _ = prompt_state.shape
        half = jnp.bfloat16
        w = plane_width(n)
        planes = n // w
        chunks = max(1, rows // 64)
        part = rows // chunks
        anywhere = pl.BlockSpec(memory_space=pl.ANY)
        scalar = pl.BlockSpec(memory_space=pltpu.SMEM)
        dma = pltpu.SemaphoreType.DMA
        regular = pltpu.SemaphoreType.REGULAR
        spread = pltpu.VMEM((planes, w, chunks, 2, part, DV), half)
        sums = pltpu.VMEM((2, w // 2, planes, rows, DV), half)
        chips = pltpu.VMEM((w // 2, planes, rows, DV), half)
        chain = pltpu.VMEM((planes, rows, DV), half)
        block = pltpu.VMEM((tokens, width), half)
        return pl.pallas_call(
            functools.partial(kernel, n),
            out_shape=pltpu.VMEM((tokens, width), half),
            in_specs=[anywhere] * 4 + [scalar] * 2,
            out_specs=pl.BlockSpec(memory_space=pltpu.VMEM),
            scratch_shapes=[
                block, block, block,
                pltpu.VMEM((count, rows, DV), half),
                pltpu.VMEM((tokens, width), jnp.float32),
                pltpu.VMEM((width // DK, DK, DV), jnp.float32),
                pltpu.VMEM((planes, chunks, lengths.shape[0], part, DV), half),
                sums, sums, chips, chips, chain, chain,
                chips, pltpu.VMEM((planes, w, rows, DV), half),
                spread, spread,
                pltpu.SMEM((2 * w + 1,), jnp.int32),
                pltpu.SMEM((2 * w + 1,), jnp.int32),
                regular, regular,
                dma((4,)), dma((planes, 2)), dma((planes, chunks)), dma((2,)), dma((2, planes)),
                dma(()), dma((w // 2, planes)),
                dma(()), dma((planes,)), dma((3,)), dma((planes, w)), dma(()), dma((planes, w)),
            ],
            compiler_params=pltpu.CompilerParams(
                collective_id=0, has_side_effects=True, vmem_limit_bytes=62 << 20),
        )(queries, keys, values, prompt_state, lengths, prompt_of.reshape(-1))

    placed = (
        P(("groups", "seq"), None),
        P(("groups", "seq"), None),
        P(("groups", "seq"), None),
        P("groups", "seq", None),
        P("groups"),
        P("groups", None),
    )
    return jax.shard_map(
        shards, mesh=mesh, in_specs=placed, out_specs=P(("groups", "seq"), None), check_vma=False
    )
```

```python
import functools
import jax
import jax.numpy as jnp
from jax import lax
from jax.experimental import pallas as pl
from jax.experimental.pallas import tpu as pltpu
from jax.sharding import PartitionSpec as P

DK = 128
DV = 128
SPAN = 128
epsilon = 1e-06


def matmul(a, b, ca, cb):
    return lax.dot_general(a, b, (((ca,), (cb,)), ((), ())), preferred_element_type=jnp.float32)


def plane_width(n):
    x = 1
    while (2 * x) ** 3 <= n // 2:
        x *= 2
    return 2 * x


def kernel(n, q_hbm, k_hbm, v_hbm, p_hbm, len_ref, of_ref, out_ref,
           q_ref, k_ref, v_ref, prompts, intra, first, gathered, t_own, t_mate, tc_out, tc_in, s_out, s_in, e_out, e_in, d_out, d_in, flag, index,
           ready_up, ready_mate, load_sem, g_send, g_recv, t_send, t_recv, tc_send, tc_recv, s_send, s_recv, e_send, e_recv, d_send, d_recv):
    me = lax.axis_index("seq")
    w = plane_width(n)
    planes = n // w
    z = me // w
    j = lax.rem(me, w)
    upper = 2 * z >= planes
    chips = w // 2
    x = j // 2
    core = lax.rem(j, 2)
    mate = me + 1 - 2 * core
    heads = k_ref.shape[1] // DK
    rows = prompts.shape[1]
    pieces = DK // rows
    per_level = w // pieces
    _, chunks, responses, part, _ = gathered.shape
    some = responses - 1

    def load(i, src, dst):
        return pltpu.make_async_copy(src, dst, load_sem.at[i])

    loads = [load(0, p_hbm, prompts), load(1, k_hbm, k_ref), load(2, v_hbm, v_ref), load(3, q_hbm, q_ref)]
    for copy in loads:
        copy.start()

    def signal(sem, device):
        pl.semaphore_signal(sem, inc=1, device_id={"seq": device}, device_id_type=pl.DeviceIdType.MESH)

    def send(src, dst, send_sem, recv_sem, target):
        return pltpu.make_async_remote_copy(
            src_ref=src, dst_ref=dst, send_sem=send_sem, recv_sem=recv_sem,
            device_id={"seq": target}, device_id_type=pl.DeviceIdType.MESH)

    def pass_by(sem, ref):
        return pltpu.make_async_copy(ref, ref, sem)

    barrier = pltpu.get_barrier_semaphore()
    has_up = z < planes - 1
    has_down = z > 0

    @pl.when(has_up)
    def _():
        signal(barrier, me + w)

    @pl.loop(j + 1, w)
    def _(m):
        signal(barrier, z * w + m)

    @pl.when(me > 0)
    def _():
        pl.semaphore_wait(barrier, j + jnp.where(has_down, 1, 0))

    @pl.when(has_down)
    def _():
        signal(ready_up, me - w)

    @pl.loop(0, j)
    def _(m):
        signal(ready_mate, z * w + m)

    def held(plane, up, f):
        if up:
            last = plane == planes - 1
            pl.when(2 * plane < planes)(lambda: f(0, responses))
            pl.when(jnp.logical_and(2 * plane >= planes, jnp.logical_not(last)))(lambda: f(1, responses - 1))
            pl.when(last)(lambda: f(2, responses - 2))
        else:
            pl.when(2 * plane < planes)(lambda: f(0, responses - 1))
            pl.when(2 * plane >= planes)(lambda: f(0, responses))

    def hop(level, c, up):
        def go(low, count):
            ref = gathered.at[level, c, pl.ds(low, count)]
            send(ref, ref, g_send.at[level, int(up)], g_recv.at[level, c], me + w if up else me - w).start()

        held(z + 1 if up else z - 1, up, go)

    def hop_sent(level, up):
        held(z + 1 if up else z - 1, up, lambda low, count: pass_by(g_send.at[level, int(up)], gathered.at[level, :, pl.ds(low, count)]).wait())

    def hop_arrived(level, c, up):
        held(z, up, lambda low, count: pass_by(g_recv.at[level, c], gathered.at[level, c, pl.ds(low, count)]).wait())

    loads[0].wait()
    for r in range(responses):
        gathered[z, :, r] = prompts[of_ref[r]].reshape(chunks, part, DV)

    @pl.when(has_down)
    def _():
        for c in range(chunks):
            hop(z, c, False)

    last = z == planes - 1

    @pl.loop(0, 2 * w + 1)
    def _(i):
        c = 2 * z * w + i
        start = jnp.int32(0)
        begins = jnp.int32(0)
        which = jnp.int32(-1)
        for r in range(responses):
            begins = begins + jnp.where(start == c, 1, 0)
            which = which + jnp.where(start <= c, 1, 0)
            start = start + len_ref[r]
        flag[i] = begins
        index[i] = which

    started = jnp.where(last, index[0] + jnp.where(flag[0] > 0, 0, 1), 0)

    @pl.when(z == 0)
    def _():
        s_in[...] = jnp.zeros_like(s_in)

    second_starts = flag[2 * j + 1] > 0

    def columns(h):
        return pl.ds(pl.multiple_of(h * DK, DK), DK)

    low = jnp.where(last, 2, jnp.where(upper, 1, 0))

    def prompt(level, c, block, floor):
        which = index[block]
        chosen = jnp.zeros((part, DV), jnp.bfloat16)
        for i in range(some):
            r = jnp.minimum(low + i, responses - 1)
            chosen = jnp.where(jnp.logical_and(which == r, which >= floor), gathered[level, c, r], chosen)
        return chosen

    def make(level, c):
        for k in range(w):
            m = lax.rem(j + k, w)
            ref = d_in.at[level, j] if k == 0 else d_out.at[level, m]
            for block in range(2):
                ref[c, block] = prompt(level, c, 2 * m + block, started)

    def give(level, c):
        for k in range(1, w):
            m = lax.rem(j + k, w)
            send(d_out.at[level, m, c], d_in.at[level, j, c], d_send, d_recv.at[level, j], z * w + m).start()

    @pl.when(j < w - 1)
    def _():
        pl.semaphore_wait(ready_mate, w - 1 - j)

    @pl.when(has_up)
    def _():
        pl.semaphore_wait(ready_up, 1)
        for c in range(chunks):
            hop(z, c, True)

    loads[1].wait()
    loads[2].wait()

    def share(level, half, number):
        send(t_own.at[half, :, level], t_mate.at[half, :, level], t_send.at[number], t_recv.at[number, level], mate).start()

    @pl.loop(0, planes)
    def _(level):
        for i in range(per_level):
            h = level * per_level + i
            cols = columns(h)
            a = matmul(k_ref[0:SPAN, cols], v_ref[0:SPAN, cols], 0, 0)
            b = matmul(k_ref[SPAN:2 * SPAN, cols], v_ref[SPAN:2 * SPAN, cols], 0, 0)
            first[h] = a
            total = jnp.where(second_starts, b, a + b).astype(jnp.bfloat16)
            for p in range(pieces):
                column = i * pieces + p
                t_own[column % 2, column // 2, level] = total[p * rows:(p + 1) * rows]
        share(level, 1 - core, 0)

    late = flag[4 * x + 2] + flag[4 * x + 3] > 0
    needed = jnp.logical_or(has_up, x < chips - 1)

    @pl.loop(0, planes)
    def _(level):
        pass_by(t_recv.at[0, level], t_mate.at[core, :, level]).wait()
        for k in range(chips):
            to = lax.rem(x + k, chips)
            column = 2 * to + core
            own = t_own[core, to, level].astype(jnp.float32)
            other = t_mate[core, to, level].astype(jnp.float32)
            total = jnp.where(late, jnp.where(core == 1, own, other), own + other).astype(jnp.bfloat16)
            if k == 0:
                tc_in[x, level] = total
            else:
                tc_out[to, level] = total

                @pl.when(needed)
                def _():
                    send(tc_out.at[to, level], tc_in.at[x, level], tc_send, tc_recv.at[x, level], z * w + column).start()

    for c in range(chunks):
        make(z, c)
        give(z, c)

    @pl.when(core == 0)
    def _():
        @pl.loop(0, planes)
        def _(level):
            share(level, 0, 1)

    loads[3].wait()
    causal = lax.broadcasted_iota(jnp.int32, (SPAN, SPAN), 0) >= lax.broadcasted_iota(jnp.int32, (SPAN, SPAN), 1)

    group = 4

    @pl.loop(0, heads, step=group)
    def _(base):
        parts = []
        for u in range(group):
            for block in range(2):
                parts.append((slice(block * SPAN, (block + 1) * SPAN), columns(base + u)))
        weights = [jnp.where(causal, matmul(q_ref[rng, cols], k_ref[rng, cols], 1, 1), 0.0).astype(jnp.bfloat16) for rng, cols in parts]
        for (rng, cols), weight in zip(parts, weights):
            intra[rng, cols] = matmul(weight, v_ref[rng, cols], 1, 0)

    def receive(level, c, up):
        hop_arrived(level, c, up)

        @pl.when(has_up if up else has_down)
        def _():
            hop(level, c, up)

    def both(distance, f):
        @pl.when(z + distance < planes)
        def _():
            f(z + distance, False)

        @pl.when(z - distance >= 0)
        def _():
            f(z - distance, True)

    def scan(level):
        for k in range(1, chips):
            other = lax.rem(x + k, chips)

            @pl.when(jnp.logical_or(has_up, other < chips - 1))
            def _():
                pass_by(tc_recv.at[other, level], tc_in.at[other, level]).wait()

        @pl.when(has_down)
        def _():
            pass_by(s_recv.at[level], s_in.at[level]).wait()

        state = s_in[level].astype(jnp.float32)
        for i in range(chips):
            state = jnp.where(flag[4 * i] > 0, 0.0, state)
            e_out[i, level] = state.astype(jnp.bfloat16)
            inside = flag[4 * i + 1] + flag[4 * i + 2] + flag[4 * i + 3]
            state = jnp.where(inside > 0, 0.0, state) + tc_in[i, level].astype(jnp.float32)

        @pl.when(z != planes - 2)
        def _():
            s_out[level] = state.astype(jnp.bfloat16)

        @pl.when(z == planes - 2)
        def _():
            for c in range(chunks):
                rng = slice(c * part, (c + 1) * part)
                s_out[level, rng] = (state[rng] + prompt(level, c, 2 * w, 0).astype(jnp.float32)).astype(jnp.bfloat16)

        @pl.when(has_up)
        def _():
            send(s_out.at[level], s_in.at[level], s_send, s_recv.at[level], me + w).start()

        for k in range(1, chips):
            to = lax.rem(x + k, chips)
            send(e_out.at[to, level], e_in.at[level, j], e_send.at[1], e_recv.at[level, j], z * w + 2 * to + core).start()
        e_in[level, j] = e_out[x, level]
        send(e_in.at[level, j], e_in.at[level, j], e_send.at[0], e_recv.at[level, j], mate).start()

    def relay(level):
        for k in range(1, chips):
            column = 2 * lax.rem(x + k, chips) + core
            pass_by(e_recv.at[level, column], e_in.at[level, column]).wait()
            send(e_in.at[level, column], e_in.at[level, column], e_send.at[2], e_recv.at[level, column], mate).start()

    def step(distance, c):
        both(distance, lambda level, up: receive(level, c, up))

        def pass_on(level, up):
            make(level, c)
            give(level, c)

        both(distance, pass_on)

    share_of = planes // chunks

    def some_levels(c, f):
        for i in range(share_of):
            f(c * share_of + i)

    def back(i):
        scan(planes - 1 - i)

    def steps(distance, before=None, after=None):
        @pl.loop(0, chunks)
        def _(c):
            if before is not None:
                pl.when(before(c))(lambda: some_levels(c, back))
            step(distance, c)
            if after is not None:
                pl.when(after(c))(lambda: some_levels(c, back))

    if planes == 4:
        steps(1, after=lambda c: z == 0)
        pl.when(z == 1)(lambda: pl.loop(0, planes)(back))
        steps(2, after=lambda c: z == 2)
    else:
        steps(1, after=lambda c: z == 0)
        steps(2, after=lambda c: jnp.logical_and(z > 0, z < planes - 2))

        @pl.loop(3, planes - 2)
        def _(distance):
            steps(distance)

        steps(planes - 2, after=lambda c: z == planes - 2)

    @pl.when(z == 0)
    def _():
        pl.loop(0, planes)(lambda i: relay(planes - 1 - i))

    steps(planes - 1, before=lambda c: last)

    fresh = jnp.logical_and(core == 1, flag[2 * j] == 0)
    open_end = jnp.logical_or(core == 0, flag[4 * x + 1] + flag[4 * x + 2] == 0)

    def finish(level, which):
        @pl.when(core == 1)
        def _():
            pass_by(t_recv.at[1, level], t_mate.at[0, :, level]).wait()

        for i in which:
            for o in range(i * pieces, (i + 1) * pieces):
                @pl.when(core != o % 2)
                def _():
                    pass_by(e_recv.at[level, o], e_in.at[level, o]).wait()

        for i in which:
            for o in range(pieces):
                owner = i * pieces + o

                @pl.when(owner != j)
                def _():
                    pass_by(d_recv.at[level, owner], d_in.at[level, owner]).wait()

        for i in which:
            cols = columns(level * per_level + i)
            entering = d_in[level, pl.ds(i * pieces, pieces), :, 0].reshape(DK, DV)
            second = d_in[level, pl.ds(i * pieces, pieces), :, 1].reshape(DK, DV)
            before = jnp.concatenate([t_mate[o % 2, o // 2, level] for o in range(i * pieces, (i + 1) * pieces)], axis=0)
            summed = e_in[level, pl.ds(i * pieces, pieces)].reshape(DK, DV).astype(jnp.float32)
            state = entering.astype(jnp.float32) + jnp.where(open_end, summed, 0.0) + jnp.where(fresh, before.astype(jnp.float32), 0.0)
            later = (state + first[level * per_level + i]).astype(jnp.bfloat16)
            at = (state.astype(jnp.bfloat16), jnp.where(second_starts, second, later))
            for block in range(2):
                rng = slice(block * SPAN, (block + 1) * SPAN)
                o = matmul(q_ref[rng, cols], at[block], 1, 0) + intra[rng, cols]
                scale = lax.rsqrt(jnp.mean(o * o, axis=-1, keepdims=True) + epsilon)
                out_ref[rng, cols] = (o * scale).astype(jnp.bfloat16)

    @pl.when(z == 0)
    def _():
        @pl.loop(0, planes)
        def _(level):
            finish(level, range(per_level))

    @pl.when(has_down)
    def _():
        ahead = 2

        @pl.loop(0, planes + ahead)
        def _(i):
            pl.when(i < planes)(lambda: relay(planes - 1 - i))
            pl.when(i >= ahead)(lambda: finish(planes - 1 + ahead - i, range(per_level)))

    pass_by(t_send.at[0], t_own.at[0]).wait()

    @pl.when(core == 0)
    def _():
        pass_by(t_send.at[1], t_own.at[0]).wait()


    @pl.when(needed)
    def _():
        pass_by(tc_send, tc_out.at[0:chips - 1]).wait()

    pass_by(e_send.at[0], s_out).wait()
    pass_by(e_send.at[1], e_out.at[0:chips - 1]).wait()
    pass_by(e_send.at[2], e_out.at[0:chips - 1]).wait()
    pass_by(d_send, d_out.at[:, 0:w - 1]).wait()

    @pl.when(has_up)
    def _():
        pass_by(s_send, s_out).wait()

        @pl.loop(0, z + 1)
        def _(level):
            hop_sent(level, True)

    @pl.when(has_down)
    def _():
        @pl.loop(z, planes)
        def _(level):
            hop_sent(level, False)


def solution(mesh):
    n = mesh.shape["seq"]

    def shards(queries, keys, values, prompt_state, lengths, prompt_of):
        tokens, width = queries.shape
        count, rows, _ = prompt_state.shape
        half = jnp.bfloat16
        w = plane_width(n)
        planes = n // w
        chunks = max(1, rows // 64)
        part = rows // chunks
        anywhere = pl.BlockSpec(memory_space=pl.ANY)
        scalar = pl.BlockSpec(memory_space=pltpu.SMEM)
        dma = pltpu.SemaphoreType.DMA
        regular = pltpu.SemaphoreType.REGULAR
        spread = pltpu.VMEM((planes, w, chunks, 2, part, DV), half)
        sums = pltpu.VMEM((2, w // 2, planes, rows, DV), half)
        chips = pltpu.VMEM((w // 2, planes, rows, DV), half)
        chain = pltpu.VMEM((planes, rows, DV), half)
        block = pltpu.VMEM((tokens, width), half)
        return pl.pallas_call(
            functools.partial(kernel, n),
            out_shape=pltpu.VMEM((tokens, width), half),
            in_specs=[anywhere] * 4 + [scalar] * 2,
            out_specs=pl.BlockSpec(memory_space=pltpu.VMEM),
            scratch_shapes=[
                block, block, block,
                pltpu.VMEM((count, rows, DV), half),
                pltpu.VMEM((tokens, width), jnp.float32),
                pltpu.VMEM((width // DK, DK, DV), jnp.float32),
                pltpu.VMEM((planes, chunks, lengths.shape[0], part, DV), half),
                sums, sums, chips, chips, chain, chain,
                chips, pltpu.VMEM((planes, w, rows, DV), half),
                spread, spread,
                pltpu.SMEM((2 * w + 1,), jnp.int32),
                pltpu.SMEM((2 * w + 1,), jnp.int32),
                regular, regular,
                dma((4,)), dma((planes, 2)), dma((planes, chunks)), dma((2,)), dma((2, planes)),
                dma(()), dma((w // 2, planes)),
                dma(()), dma((planes,)), dma((3,)), dma((planes, w)), dma(()), dma((planes, w)),
            ],
            compiler_params=pltpu.CompilerParams(
                collective_id=0, has_side_effects=True, vmem_limit_bytes=62 << 20),
        )(queries, keys, values, prompt_state, lengths, prompt_of.reshape(-1))

    placed = (
        P(("groups", "seq"), None),
        P(("groups", "seq"), None),
        P(("groups", "seq"), None),
        P("groups", "seq", None),
        P("groups"),
        P("groups", None),
    )
    return jax.shard_map(
        shards, mesh=mesh, in_specs=placed, out_specs=P(("groups", "seq"), None), check_vma=False
    )
```
